32 devices in a mesh: dp: 8 (over z, y), row: 2 (over core), col: 2 (over x).
Axes of the slice: x: 2, y: 2, z: 4, core: 2. Of those that a mesh axis runs over, the one named last changes fastest.
Arguments:
- hidden_in: bfloat16 [4096, 960], P(('dp', 'col'), 'row')
- segment_ids: int32 [4096], P('dp'), may hold values from 0 to 4095, as said below
- position_ids: int32 [4096], P('dp'), may hold values from 0 to 2048, as said below
- attn_gain: float32 [960], P('row'), may hold values from 0.5 to 1.5
- query_weight: bfloat16 [960, 960], P('row', 'col')
- key_weight: bfloat16 [960, 320], P('row', 'col')
- value_matrix: bfloat16 [960, 320], P('row', 'col'), may hold values from -0.1875 to 0.1875
- output_weight: bfloat16 [960, 960], P('col', 'row'), may hold values from -0.75 to 0.75
- ffn_gain: float32 [960], P('row'), may hold values from 0.5 to 1.5
- gate_weight: bfloat16 [960, 2560], P('row', 'col'), may hold values from -0.1875 to 0.1875
- up_weight: bfloat16 [960, 2560], P('row', 'col'), may hold values from -0.1875 to 0.1875
- down_weight: bfloat16 [2560, 960], P('col', 'row'), may hold values from -0.125 to 0.125
- out_grad: bfloat16 [4096, 960], P(('dp', 'col'), 'row')
Outputs:
- hidden_out: bfloat16 [4096, 960], P(('dp', 'col'), 'row')
- hidden_in_grad: float32 [4096, 960], P(('dp', 'col'), 'row')
- attn_gain_grad: float32 [960], P('row')
- query_weight_grad: float32 [960, 960], P('row', 'col')
- key_weight_grad: float32 [960, 320], P('row', 'col')
- value_weight_grad: float32 [960, 320], P('row', 'col')
- output_weight_grad: float32 [960, 960], P('col', 'row')
- ffn_gain_grad: float32 [960], P('row')
- gate_weight_grad: float32 [2, 960, 1280], P('col', 'row', 'dp')
- up_weight_grad: float32 [2, 960, 1280], P('col', 'row', 'dp')
- down_weight_grad: float32 [2, 1280, 960], P('col', 'dp', 'row')
The draws below stay inside these ranges and needn't reach their ends.
Inputs may be any that keep to these rules, and one draw needn't show every extreme that they name: `segment_ids`: segment numbers never fall from one token to the next, and the first token of each sequence of 512 tokens begins a new number. `position_ids`: within a document each token's position is one or two more than the previous token's; the first token of each sequence of 512 tokens has position 0.
All inputs are finite; a program needn't handle non-finite values.
Results may differ from the reference program's by a relative error of at most 0.02.
The reference program's roundings to bfloat16 on the way count: a program that leaves them out, or rounds other values in their place, can miss the bound.
Values may be sent and summed in bfloat16 or wider, within the bound.
A program may use at most 128 MiB of HBM per device.

```python
import math
import jax
import jax.numpy as jnp
from jax import lax

MODEL_WIDTH = 960
QUERY_HEADS = 15
KEY_VALUE_HEADS = 5
HEAD_SIZE = 64
FEEDFWD_UNITS = 2560
PACKED_TOKENS = 512
TOKENS = 4096
N_COL = 2


def spread_factor(key, shape, lower, upper):
    return jnp.exp(jax.random.uniform(key, shape, jnp.float32, math.log(lower), math.log(upper)))


def document_layout(key):
    key_a, second_random_key, key_c = jax.random.split(jax.random.fold_in(key, 11), 3)
    token_index = jnp.arange(TOKENS, dtype=jnp.int32)
    within = token_index % PACKED_TOKENS
    final_token = token_index == TOKENS - 1
    starts = (jax.random.randint(key_a, (TOKENS,), 0, max(PACKED_TOKENS // 2, 2)) == 0) | (within == 0) | final_token
    doc_start = lax.cummax(jnp.where(starts, token_index, 0), axis=0)
    step_sizes = jax.random.randint(second_random_key, (TOKENS,), 1, 3)
    climbed = jnp.cumsum(step_sizes) - step_sizes
    offsets = jnp.where(within == 0, 0, jax.random.randint(key_c, (TOKENS,), 0, 1024))
    offsets = jnp.where(final_token, 1024 + 2 * PACKED_TOKENS, offsets)
    position = offsets[doc_start] + climbed - climbed[doc_start]
    return (doc_start.astype(jnp.int32), position.astype(jnp.int32))


def draw_segment_ids(key, part):
    return document_layout(key)[0]


def draw_position_ids(key, part):
    return document_layout(key)[1]


def draw_query_weight(key, part):
    second_random_key = jax.random.fold_in(key, 1)
    rotary_base = jnp.clip(jax.random.normal(second_random_key, (MODEL_WIDTH, MODEL_WIDTH), jnp.float32), -6.0, 6.0) * MODEL_WIDTH ** (-0.5)
    return rotary_base.astype(jnp.bfloat16)


def draw_key_weight(key, part):
    second_random_key = jax.random.fold_in(key, 2)
    rotary_base = jnp.clip(jax.random.normal(second_random_key, (MODEL_WIDTH, KEY_VALUE_HEADS * HEAD_SIZE), jnp.float32), -6.0, 6.0) * MODEL_WIDTH ** (-0.5)
    return rotary_base.astype(jnp.bfloat16)


def draw_hidden_in(key, part):
    key_a, second_random_key, key_c = jax.random.split(jax.random.fold_in(key, 3), 3)
    rotary_base = jnp.clip(jax.random.normal(key_a, (TOKENS, MODEL_WIDTH), jnp.float32), -6.0, 6.0)
    ramp = jnp.exp(math.log(3.0) * jnp.arange(MODEL_WIDTH, dtype=jnp.float32) / MODEL_WIDTH)
    column = ramp * spread_factor(second_random_key, (MODEL_WIDTH,), 0.5, 2.0)
    row_scale = spread_factor(key_c, (TOKENS, 1), 0.3, 3.0)
    return (rotary_base * column[None, :] * row_scale).astype(jnp.bfloat16)


def draw_out_grad(key, part):
    key_a, second_random_key = jax.random.split(jax.random.fold_in(key, 4), 2)
    rotary_base = jnp.clip(jax.random.normal(key_a, (TOKENS, MODEL_WIDTH), jnp.float32), -6.0, 6.0)
    ramp = jnp.exp(math.log(3.0) * jnp.arange(TOKENS, dtype=jnp.float32) / TOKENS)
    row_scale = ramp[:, None] * spread_factor(second_random_key, (TOKENS, 1), 0.6, 1.6)
    return (rotary_base * row_scale).astype(jnp.bfloat16)


def levels(rng, dims, shards, low, high):
    level = 1.0
    for dim, blocks in shards:
        steps = jax.random.uniform(jax.random.fold_in(jax.random.fold_in(rng, 6), dim), (blocks,), jnp.float32, low / len(shards), high / len(shards))
        level = level * jnp.repeat(jnp.exp(steps), dims[dim] // blocks).reshape((-1,) + (1,) * (len(dims) - 1 - dim))
    return level


def scatter_about(own_key, dims, spread, limit, pieces=(), held_as=jnp.bfloat16):
    result = spread * jax.random.normal(own_key, dims, jnp.float32)
    if pieces:
        result = result * levels(own_key, dims, pieces, -0.22, 0.18)
    return jnp.clip(result, -limit, limit).astype(held_as)


def setup_inputs(seed: int = 0) -> dict:
    arg_keys = jax.random.split(jax.random.key(seed), 14)
    return {
        "hidden_in": draw_hidden_in(jax.random.fold_in(arg_keys[13], 71), 0),
        "segment_ids": draw_segment_ids(jax.random.fold_in(arg_keys[13], 71), 0),
        "position_ids": draw_position_ids(jax.random.fold_in(arg_keys[13], 71), 0),
        "attn_gain": jnp.clip(1.0 + 0.1 * jax.random.normal(arg_keys[3], (MODEL_WIDTH,), jnp.float32), 0.5, 1.5),
        "query_weight": draw_query_weight(jax.random.fold_in(arg_keys[13], 71), 0),
        "key_weight": draw_key_weight(jax.random.fold_in(arg_keys[13], 71), 0),
        "value_matrix": scatter_about(arg_keys[6], (MODEL_WIDTH, KEY_VALUE_HEADS * HEAD_SIZE), MODEL_WIDTH ** -0.5, 0.1875, ((0, 2), (1, 2))),
        "output_weight": scatter_about(arg_keys[7], (MODEL_WIDTH, MODEL_WIDTH), (MODEL_WIDTH // 16) ** -0.5, 0.75, ((0, 2), (1, 2))),
        "ffn_gain": jnp.clip(1.0 + 0.1 * jax.random.normal(arg_keys[8], (MODEL_WIDTH,), jnp.float32), 0.5, 1.5),
        "gate_weight": scatter_about(arg_keys[9], (MODEL_WIDTH, FEEDFWD_UNITS), MODEL_WIDTH ** -0.5, 0.1875, ((0, 2), (1, 2))),
        "up_weight": scatter_about(arg_keys[10], (MODEL_WIDTH, FEEDFWD_UNITS), MODEL_WIDTH ** -0.5, 0.1875, ((0, 2), (1, 2))),
        "down_weight": scatter_about(arg_keys[11], (FEEDFWD_UNITS, MODEL_WIDTH), FEEDFWD_UNITS ** -0.5, 0.125, ((0, 2), (1, 2))),
        "out_grad": draw_out_grad(jax.random.fold_in(arg_keys[13], 71), 0),
    }


epsilon = 1e-05
rope_base = 10000.0
masked_score = -1e+30

def rounded_values(values):
    return lax.optimization_barrier(values.astype(jnp.bfloat16))

def rope_tables(position_row):
    half_size = HEAD_SIZE // 2
    frequency = rope_base ** (-(jnp.arange(half_size, dtype=jnp.float32) * 2.0) / HEAD_SIZE)
    angles = position_row.astype(jnp.float32)[:, None] * frequency[None, :]
    return (jnp.cos(angles), jnp.sin(angles))

def apply_rotary(values, cosine_table, sine_lookup, direction):
    half_size = values.shape[-1] // 2
    front_half = values[..., :half_size]
    back_half = values[..., half_size:]
    cosine_wide = cosine_table[:, None, :]
    sine_wide = direction * sine_lookup[:, None, :]
    return jnp.concatenate([front_half * cosine_wide - back_half * sine_wide, back_half * cosine_wide + front_half * sine_wide], axis=-1)

def norm_forward(residual, gain):
    mean_square = lax.optimization_barrier(jnp.mean(residual * residual, axis=1))
    inverse_rms = lax.rsqrt(mean_square + epsilon)
    unit_rows = residual * inverse_rms[:, None]
    return (unit_rows, inverse_rms, rounded_values(unit_rows * gain[None, :]))

def norm_backward(grad_normed, unit_rows, inverse_rms, gain):
    weighted = grad_normed * gain[None, :]
    inner_mean = lax.optimization_barrier(jnp.mean(weighted * unit_rows, axis=1))
    grad_input = inverse_rms[:, None] * (weighted - unit_rows * inner_mean[:, None])
    return (grad_input, lax.optimization_barrier(jnp.sum(grad_normed * unit_rows, axis=0)))

def matmul(left, right):
    return jnp.dot(left, right, preferred_element_type=jnp.float32)

def layer_pass(weights, hidden_rows, grad_rows, segment_row, position_row):
    attn_gain, query_weight, key_weight, value_matrix, output_weight, ffn_gain, gate_weight, up_weight, down_weight = weights
    heads_per_group = QUERY_HEADS // KEY_VALUE_HEADS
    score_scale = HEAD_SIZE ** (-0.5)
    residual = hidden_rows.astype(jnp.float32)
    unit_one, inverse_one, normed_one = norm_forward(residual, attn_gain)
    query = rounded_values(matmul(normed_one, query_weight))
    key = rounded_values(matmul(normed_one, key_weight))
    value_states = rounded_values(matmul(normed_one, value_matrix))
    cosine_table, sine_lookup = rope_tables(position_row)
    query_rotated = rounded_values(apply_rotary(query.astype(jnp.float32).reshape(PACKED_TOKENS, QUERY_HEADS, HEAD_SIZE), cosine_table, sine_lookup, 1.0))
    key_rotated = rounded_values(apply_rotary(key.astype(jnp.float32).reshape(PACKED_TOKENS, KEY_VALUE_HEADS, HEAD_SIZE), cosine_table, sine_lookup, 1.0))
    token_index = jnp.arange(PACKED_TOKENS, dtype=jnp.int32)
    allowed = (segment_row[:, None] == segment_row[None, :]) & (token_index[None, :] <= token_index[:, None])
    query_group = query_rotated.reshape(PACKED_TOKENS, KEY_VALUE_HEADS, heads_per_group, HEAD_SIZE).astype(jnp.float32)
    key_group = key_rotated.reshape(PACKED_TOKENS, KEY_VALUE_HEADS, HEAD_SIZE).astype(jnp.float32)
    value_group = value_states.reshape(PACKED_TOKENS, KEY_VALUE_HEADS, HEAD_SIZE).astype(jnp.float32)
    scores = jnp.einsum('qkgd,skd->kgqs', query_group, key_group) * score_scale
    scores = jnp.where(allowed[None, None], scores, masked_score)
    row_max = lax.optimization_barrier(jnp.max(scores, axis=-1, keepdims=True))
    log_total = row_max + jnp.log(lax.optimization_barrier(jnp.sum(jnp.exp(scores - row_max), axis=-1, keepdims=True)))
    prob_exact = jnp.exp(scores - log_total)
    attn_probs = rounded_values(prob_exact).astype(jnp.float32)
    attended_output = rounded_values(jnp.einsum('kgqs,skd->qkgd', attn_probs, value_group)).reshape(PACKED_TOKENS, MODEL_WIDTH)
    mid = residual + matmul(attended_output, output_weight)
    unit_two, inverse_two, normed_two = norm_forward(mid, ffn_gain)
    gate_pre = matmul(normed_two, gate_weight)
    up_pre = matmul(normed_two, up_weight)
    gate_sigmoid = jax.nn.sigmoid(gate_pre)
    gate_silu = gate_pre * gate_sigmoid
    inner_act = rounded_values(gate_silu * up_pre)
    final = mid + matmul(inner_act, down_weight)
    hidden_out = final.astype(jnp.bfloat16)
    down_wgrad = matmul(inner_act.T, grad_rows)
    inner_grad = matmul(grad_rows, down_weight.T)
    silu_slope = gate_sigmoid * (1.0 + gate_pre * (1.0 - gate_sigmoid))
    gate_grad = rounded_values(inner_grad * up_pre * silu_slope)
    up_grad = rounded_values(inner_grad * gate_silu)
    gate_wgrad = matmul(normed_two.T, gate_grad)
    up_wgrad = matmul(normed_two.T, up_grad)
    normed_two_grad = matmul(gate_grad, gate_weight.T) + matmul(up_grad, up_weight.T)
    mid_part, ffn_gain_part = norm_backward(normed_two_grad, unit_two, inverse_two, ffn_gain)
    mid_grad = grad_rows.astype(jnp.float32) + mid_part
    mid_grad_bf = rounded_values(mid_grad)
    out_wgrad = matmul(attended_output.T, mid_grad_bf)
    attended_gradient = rounded_values(matmul(mid_grad_bf, output_weight.T))
    gradient_group = attended_gradient.reshape(PACKED_TOKENS, KEY_VALUE_HEADS, heads_per_group, HEAD_SIZE).astype(jnp.float32)
    attended_group = attended_output.reshape(PACKED_TOKENS, KEY_VALUE_HEADS, heads_per_group, HEAD_SIZE).astype(jnp.float32)
    grad_dot = jnp.transpose(lax.optimization_barrier(jnp.sum(gradient_group * attended_group, axis=-1)), (1, 2, 0))
    value_gradient = jnp.einsum('kgqs,qkgd->skd', attn_probs, gradient_group)
    prob_grad = jnp.einsum('qkgd,skd->kgqs', gradient_group, value_group)
    score_grad = rounded_values(prob_exact * (prob_grad - grad_dot[..., None]) * score_scale).astype(jnp.float32)
    query_grad = jnp.einsum('kgqs,skd->qkgd', score_grad, key_group)
    key_gradient = jnp.einsum('kgqs,qkgd->skd', score_grad, query_group)
    query_back = rounded_values(apply_rotary(query_grad.reshape(PACKED_TOKENS, QUERY_HEADS, HEAD_SIZE), cosine_table, sine_lookup, -1.0)).reshape(PACKED_TOKENS, MODEL_WIDTH)
    key_backward = rounded_values(apply_rotary(key_gradient, cosine_table, sine_lookup, -1.0)).reshape(PACKED_TOKENS, KEY_VALUE_HEADS * HEAD_SIZE)
    value_backward = rounded_values(value_gradient).reshape(PACKED_TOKENS, KEY_VALUE_HEADS * HEAD_SIZE)
    query_wgrad = matmul(normed_one.T, query_back)
    key_wgrad = matmul(normed_one.T, key_backward)
    value_wgrad = matmul(normed_one.T, value_backward)
    normed_one_grad = matmul(query_back, query_weight.T) + matmul(key_backward, key_weight.T) + matmul(value_backward, value_matrix.T)
    in_part, attn_gain_part = norm_backward(normed_one_grad, unit_one, inverse_one, attn_gain)
    hidden_in_grad = mid_grad + in_part
    grads = (attn_gain_part, query_wgrad, key_wgrad, value_wgrad, out_wgrad, ffn_gain_part, gate_wgrad, up_wgrad, down_wgrad)
    return (hidden_out, hidden_in_grad, grads)

def reference(hidden_in, segment_ids, position_ids, attn_gain, query_weight, key_weight, value_matrix, output_weight, ffn_gain, gate_weight, up_weight, down_weight, out_grad):
    seq_count = hidden_in.shape[0] // PACKED_TOKENS
    weights = (attn_gain, query_weight, key_weight, value_matrix, output_weight, ffn_gain, gate_weight, up_weight, down_weight)
    sequence_items = (hidden_in.reshape(seq_count, PACKED_TOKENS, MODEL_WIDTH), out_grad.reshape(seq_count, PACKED_TOKENS, MODEL_WIDTH), segment_ids.reshape(seq_count, PACKED_TOKENS), position_ids.reshape(seq_count, PACKED_TOKENS))
    initial_gradients = (jnp.zeros((MODEL_WIDTH,), jnp.float32), jnp.zeros((MODEL_WIDTH, MODEL_WIDTH), jnp.float32), jnp.zeros((MODEL_WIDTH, KEY_VALUE_HEADS * HEAD_SIZE), jnp.float32), jnp.zeros((MODEL_WIDTH, KEY_VALUE_HEADS * HEAD_SIZE), jnp.float32), jnp.zeros((MODEL_WIDTH, MODEL_WIDTH), jnp.float32), jnp.zeros((MODEL_WIDTH,), jnp.float32), jnp.zeros((MODEL_WIDTH, FEEDFWD_UNITS), jnp.float32), jnp.zeros((MODEL_WIDTH, FEEDFWD_UNITS), jnp.float32), jnp.zeros((FEEDFWD_UNITS, MODEL_WIDTH), jnp.float32))

    def one_sequence(totals, items):
        hidden_out, hidden_in_grad, grads = layer_pass(weights, items[0], items[1], items[2], items[3])
        new_totals = tuple((total + grad for total, grad in zip(totals, grads)))
        return (new_totals, (hidden_out, hidden_in_grad))
    totals, (outputs, input_grads) = lax.scan(one_sequence, initial_gradients, sequence_items)
    gate_total = totals[6].reshape(MODEL_WIDTH, N_COL, FEEDFWD_UNITS // N_COL).transpose(1, 0, 2)
    up_total = totals[7].reshape(MODEL_WIDTH, N_COL, FEEDFWD_UNITS // N_COL).transpose(1, 0, 2)
    down_total = totals[8].reshape(N_COL, FEEDFWD_UNITS // N_COL, MODEL_WIDTH)
    return (outputs.reshape(seq_count * PACKED_TOKENS, MODEL_WIDTH), input_grads.reshape(seq_count * PACKED_TOKENS, MODEL_WIDTH), totals[0], totals[1], totals[2], totals[3], totals[4], totals[5], gate_total, up_total, down_total)
```

```python
import functools

import jax
import jax.numpy as jnp
from jax import lax
from jax.experimental import pallas as pl
from jax.experimental.pallas import tpu as pltpu
from jax.sharding import PartitionSpec as P

HEAD_SIZE = 64
QUERY_HEADS = 15
KEY_VALUE_HEADS = 5
epsilon = 1e-05
rope_base = 10000.0
masked_score = -1e30
MESH = pl.DeviceIdType.MESH
F32 = jnp.float32
BF16 = jnp.bfloat16
VM = pl.BlockSpec(memory_space=pltpu.VMEM)


def matmul(left, right):
    return jnp.dot(left, right, preferred_element_type=F32)


def contract_rows(left, right):
    return lax.dot_general(left, right, (((0,), (0,)), ((), ())), preferred_element_type=F32)


def contract_cols(left, right):
    return lax.dot_general(left, right, (((1,), (1,)), ((), ())), preferred_element_type=F32)


def greet(axes):
    barrier = pltpu.get_barrier_semaphore()
    for axis in axes:
        other = 1 - lax.axis_index(axis)
        pl.semaphore_signal(barrier, inc=1, device_id={axis: other}, device_id_type=MESH)
    pl.semaphore_wait(barrier, len(axes))


def remote(src, dst, send_sem, recv_sem, axis):
    return pltpu.make_async_remote_copy(
        src_ref=src,
        dst_ref=dst,
        send_sem=send_sem,
        recv_sem=recv_sem,
        device_id={axis: 1 - lax.axis_index(axis)},
        device_id_type=MESH,
    )


def call(body, outs, scratch, args, cid, vmem=60 * 2**20):
    return pl.pallas_call(
        body,
        out_shape=outs,
        in_specs=[VM] * len(args),
        out_specs=[VM] * len(outs),
        scratch_shapes=scratch,
        compiler_params=pltpu.CompilerParams(
            collective_id=cid, has_side_effects=cid is not None, vmem_limit_bytes=vmem
        ),
    )(*args)


def exchange(kinds, arrays, cid):
    n = len(arrays)

    def body(*refs):
        ins, outs, sems = refs[:n], refs[n : 2 * n], refs[2 * n]
        r, c = lax.axis_index("row"), lax.axis_index("col")
        greet(("row", "col") if "all" in kinds else ("row",))
        pending, firsts = [], []
        for i, kind in enumerate(kinds):
            if kind == "all":
                cp = remote(ins[i], outs[i].at[c, r], sems.at[i, 0], sems.at[i, 1], "col")
                cp.start()
                firsts.append((i, cp))
        for i, kind in enumerate(kinds):
            if kind == "all":
                src, keep, dst = ins[i], ins[i], outs[i].at[c, r]
            elif kind == "row":
                src, keep, dst = ins[i], ins[i], outs[i].at[r]
            elif kind == "lead":
                src, keep, dst = ins[i].at[1 - r], ins[i].at[r], outs[i].at[r]
            else:
                w = ins[i].shape[1] // 2
                src = ins[i].at[:, pl.ds(pl.multiple_of((1 - r) * w, 128), w)]
                keep = ins[i].at[:, pl.ds(pl.multiple_of(r * w, 128), w)]
                dst = outs[i].at[r]
            cp = remote(src, dst, sems.at[i, 2], sems.at[i, 3], "row")
            cp.start()
            loc = pltpu.make_async_copy(keep, dst, sems.at[i, 6])
            loc.start()
            pending += [cp, loc]
        for i, cp in firsts:
            cp.wait_recv()
            fw = remote(
                outs[i].at[1 - c, r], outs[i].at[1 - c, r], sems.at[i, 4], sems.at[i, 5], "row"
            )
            fw.start()
            pending.append(fw)
        for _, cp in firsts:
            cp.wait_send()
        for cp in pending:
            cp.wait()

    outs = []
    for kind, a in zip(kinds, arrays):
        if kind == "all":
            s = (2, 2) + a.shape
        elif kind == "row":
            s = (2,) + a.shape
        elif kind == "lead":
            s = a.shape
        else:
            s = (2, a.shape[0], a.shape[1] // 2)
        outs.append(jax.ShapeDtypeStruct(s, a.dtype))
    return call(body, outs, [pltpu.SemaphoreType.DMA((n, 7))], arrays, cid)


def scatter_scratch(part):
    s, d = part.shape[2:], part.dtype
    return [
        pltpu.VMEM((2,) + s, d),
        pltpu.VMEM(s, d),
        pltpu.VMEM(s, d),
        pltpu.SemaphoreType.DMA((6,)),
    ]


def scatter_sum(part, land, out_x, land_x, sems):
    r, c = lax.axis_index("row"), lax.axis_index("col")
    first = remote(part.at[1 - c, 1 - r], land.at[0], sems.at[0], sems.at[1], "row")
    second = remote(part.at[c, 1 - r], land.at[1], sems.at[2], sems.at[3], "row")
    first.start()
    second.start()
    first.wait_recv()
    out_x[...] = (part[1 - c, r].astype(F32) + land[0].astype(F32)).astype(out_x.dtype)
    third = remote(out_x, land_x, sems.at[4], sems.at[5], "col")
    third.start()
    second.wait_recv()
    mine = part[c, r].astype(F32) + land[1].astype(F32)
    third.wait_recv()
    total = mine + land_x[...].astype(F32)

    def finish():
        first.wait_send()
        second.wait_send()
        third.wait_send()

    return total, finish


def reduce_out(part, resid, cid):
    def body(part, resid, out, land, out_x, land_x, sems):
        greet(("row", "col"))
        total, finish = scatter_sum(part, land, out_x, land_x, sems)
        out[...] = (total + resid[...]).astype(BF16)
        finish()

    outs = [jax.ShapeDtypeStruct(resid.shape, BF16)]
    return call(body, outs, scatter_scratch(part), [part, resid], cid)[0]


def norm_back(grad, resid, gain):
    width = resid.shape[1]
    inv = lax.rsqrt(jnp.sum(resid * resid, axis=1, keepdims=True) / width + epsilon)
    unit = resid * inv
    weighted = grad * gain
    mean = jnp.sum(weighted * unit, axis=1, keepdims=True) / width
    return inv * (weighted - unit * mean), jnp.sum(grad * unit, axis=0, keepdims=True)


def mid_back(part, mid, og, gain, cid):
    def body(part, mid, og, gain, mg, mg_all, gg, land, out_x, land_x, sems, sems2):
        r, c = lax.axis_index("row"), lax.axis_index("col")
        greet(("row", "col"))
        total, finish = scatter_sum(part, land, out_x, land_x, sems)
        back, gsum = norm_back(total, mid[...], gain[...])
        back = back + og[...].astype(F32)
        mg_all[c, r] = back.astype(BF16)
        mine = mg_all.at[c, r]
        a = remote(mine, mine, sems2.at[0], sems2.at[1], "col")
        b = remote(mine, mine, sems2.at[2], sems2.at[3], "row")
        a.start()
        b.start()
        mg[...] = back
        gg[...] = gsum
        a.wait_recv()
        theirs = mg_all.at[1 - c, r]
        f = remote(theirs, theirs, sems2.at[4], sems2.at[5], "row")
        f.start()
        a.wait_send()
        b.wait()
        f.wait()
        finish()

    t, w = mid.shape
    outs = [
        jax.ShapeDtypeStruct((t, w), F32),
        jax.ShapeDtypeStruct((2, 2, t, w), BF16),
        jax.ShapeDtypeStruct((1, w), F32),
    ]
    scratch = scatter_scratch(part) + [pltpu.SemaphoreType.DMA((6,))]
    return call(body, outs, scratch, [part, mid, og, gain], cid)


def in_back(part, hid, mg, gain, cid):
    def body(part, hid, mg, gain, out, gg, land, out_x, land_x, sems, swap, got, sems2):
        r, c = lax.axis_index("row"), lax.axis_index("col")
        greet(("row", "col"))
        total, finish = scatter_sum(part, land, out_x, land_x, sems)
        back, gsum = norm_back(total, hid[...].astype(F32), gain[...])
        back = back + mg[...]
        w = back.shape[1] // 2
        swap[0] = back[:, :w]
        swap[1] = back[:, w:]
        a = remote(swap.at[1 - r], got, sems2.at[0], sems2.at[1], "row")
        a.start()
        gg[...] = gsum
        out[r] = swap[r]
        a.wait()
        out[1 - r] = got[...]
        finish()

    t, w = hid.shape
    outs = [jax.ShapeDtypeStruct((2, t, w // 2), F32), jax.ShapeDtypeStruct((1, w), F32)]
    scratch = scatter_scratch(part) + [
        pltpu.VMEM((2, t, w // 2), F32),
        pltpu.VMEM((t, w // 2), F32),
        pltpu.SemaphoreType.DMA((2,)),
    ]
    return call(body, outs, scratch, [part, hid, mg, gain], cid)


def head(values, h):
    return values[:, h * HEAD_SIZE : (h + 1) * HEAD_SIZE]


def turn(x, xp, cos, sin):
    x, xp = x.astype(F32), xp.astype(F32)
    return (x * cos + xp * sin).astype(BF16), (xp * cos - x * sin).astype(BF16)


def pick(flag, a, b):
    return jnp.where(flag, b, a)


def attn_forward(q, k, v, qp, kp, cos, sin, seg_col, seg_row, sel):
    heads = q.shape[1] // HEAD_SIZE
    t = q.shape[0]

    def body(sel, q, k, v, qp, kp, cos, sin, seg_c, seg_r, out, lt, qr, qrp, kr, krp):
        co, si = cos[...], sin[...]
        at = lax.broadcasted_iota(jnp.int32, (t, t), 0)
        to = lax.broadcasted_iota(jnp.int32, (t, t), 1)
        allowed = (seg_c[...] == seg_r[...]) & (to <= at)
        kk = []
        for g in range(2):
            a, b = turn(head(k, g), head(kp, g), co, si)
            kr[:, g * HEAD_SIZE : (g + 1) * HEAD_SIZE] = a
            krp[:, g * HEAD_SIZE : (g + 1) * HEAD_SIZE] = b
            kk.append(a)
        vv = [head(v, 0), head(v, 1)]
        for h in range(heads):
            a, b = turn(head(q, h), head(qp, h), co, si)
            qr[:, h * HEAD_SIZE : (h + 1) * HEAD_SIZE] = a
            qrp[:, h * HEAD_SIZE : (h + 1) * HEAD_SIZE] = b
            f = sel[h] == 1
            s = contract_cols(a, pick(f, *kk)) * HEAD_SIZE**-0.5
            s = jnp.where(allowed, s, masked_score)
            m = jnp.max(s, axis=1, keepdims=True)
            l = m + jnp.log(jnp.sum(jnp.exp(s - m), axis=1, keepdims=True))
            lt[:, h : h + 1] = l
            p = jnp.exp(s - l).astype(BF16)
            out[:, h * HEAD_SIZE : (h + 1) * HEAD_SIZE] = matmul(p, pick(f, *vv)).astype(BF16)

    outs = [
        jax.ShapeDtypeStruct(q.shape, BF16),
        jax.ShapeDtypeStruct((t, heads), F32),
        jax.ShapeDtypeStruct(q.shape, BF16),
        jax.ShapeDtypeStruct(q.shape, BF16),
        jax.ShapeDtypeStruct(k.shape, BF16),
        jax.ShapeDtypeStruct(k.shape, BF16),
    ]
    return pl.pallas_call(
        body,
        out_shape=outs,
        in_specs=[pl.BlockSpec(memory_space=pltpu.SMEM)] + [VM] * 9,
        out_specs=[VM] * 6,
        compiler_params=pltpu.CompilerParams(vmem_limit_bytes=60 * 2**20),
        name="attn_forward",
    )(sel, q, k, v, qp, kp, cos, sin, seg_col, seg_row)


def attn_backward(qr, qrp, kr, krp, v, lt, att, da, cos, sin, seg_col, seg_row, sel):
    heads = qr.shape[1] // HEAD_SIZE
    t = qr.shape[0]
    kw = kr.shape[1]

    def body(sel, qr, qrp, kr, krp, v, lt, att, da, cos, sin, seg_c, seg_r, out):
        co, si = cos[...], sin[...]
        at = lax.broadcasted_iota(jnp.int32, (t, t), 0)
        to = lax.broadcasted_iota(jnp.int32, (t, t), 1)
        allowed = (seg_c[...] == seg_r[...]) & (to <= at)
        kk = [jnp.concatenate([head(kr, g), head(krp, g)], axis=1) for g in range(2)]
        vv = [head(v, 0), head(v, 1)]
        dk = [jnp.zeros((t, 2 * HEAD_SIZE), F32)] * 2
        dv = [jnp.zeros((t, HEAD_SIZE), F32)] * 2
        for h in range(heads):
            f = sel[h] == 1
            kc = pick(f, *kk)
            vh = pick(f, *vv)
            qh = head(qr, h)
            dh = head(da, h)
            s = contract_cols(qh, kc[:, :HEAD_SIZE]) * HEAD_SIZE**-0.5
            s = jnp.where(allowed, s, masked_score)
            p = jnp.exp(s - lt[:, h : h + 1])
            dot = jnp.sum(dh.astype(F32) * head(att, h).astype(F32), axis=1, keepdims=True)
            dvh = contract_rows(p.astype(BF16), dh)
            dp = contract_cols(dh, vh)
            ds = (p * (dp - dot) * HEAD_SIZE**-0.5).astype(BF16)
            dq = matmul(ds, kc)
            dq = dq[:, :HEAD_SIZE] * co - dq[:, HEAD_SIZE:] * si
            out[:, h * HEAD_SIZE : (h + 1) * HEAD_SIZE] = dq.astype(BF16)
            dkh = contract_rows(ds, jnp.concatenate([qh, head(qrp, h)], axis=1))
            zk, zv = jnp.zeros_like(dkh), jnp.zeros_like(dvh)
            dk = [dk[0] + pick(f, dkh, zk), dk[1] + pick(f, zk, dkh)]
            dv = [dv[0] + pick(f, dvh, zv), dv[1] + pick(f, zv, dvh)]
        base = heads * HEAD_SIZE
        for g in range(2):
            lo = base + g * HEAD_SIZE
            back = dk[g][:, :HEAD_SIZE] * co - dk[g][:, HEAD_SIZE:] * si
            out[:, lo : lo + HEAD_SIZE] = back.astype(BF16)
            out[:, lo + kw : lo + kw + HEAD_SIZE] = dv[g].astype(BF16)

    return pl.pallas_call(
        body,
        out_shape=jax.ShapeDtypeStruct((t, heads * HEAD_SIZE + 2 * kw), BF16),
        in_specs=[pl.BlockSpec(memory_space=pltpu.SMEM)] + [VM] * 12,
        out_specs=VM,
        compiler_params=pltpu.CompilerParams(vmem_limit_bytes=60 * 2**20),
        name="attn_backward",
    )(sel, qr, qrp, kr, krp, v, lt, att, da, cos, sin, seg_col, seg_row)


def swap_halves(weights):
    w = weights.reshape(weights.shape[0], -1, 2, HEAD_SIZE // 2)
    return jnp.concatenate([-w[:, :, 1:], w[:, :, :1]], axis=2).reshape(weights.shape)


def flat(slots):
    a, b, t, w = slots.shape
    return jnp.transpose(slots, (0, 2, 1, 3)).reshape(a * t, b * w)


def ordered(r, mine, theirs, axis):
    return jnp.where(
        r == 0,
        jnp.concatenate([mine, theirs], axis=axis),
        jnp.concatenate([theirs, mine], axis=axis),
    )


PAIR = [(0, 1), (1, 0)]


def on_device(
    hidden_in,
    segment_ids,
    position_ids,
    attn_gain,
    query_weight,
    key_weight,
    value_matrix,
    output_weight,
    ffn_gain,
    gate_weight,
    up_weight,
    down_weight,
    out_grad,
):
    r, c = lax.axis_index("row"), lax.axis_index("col")
    t = segment_ids.shape[0]
    width = 2 * hidden_in.shape[1]
    qc, kc = query_weight.shape[1], key_weight.shape[1]
    half = qc % HEAD_SIZE
    fw = gate_weight.shape[1] // 2
    slots_q = (qc + half) // 2
    slots_k = 2 * HEAD_SIZE

    def edge_of(w):
        n = w.shape[1]
        return jnp.where(c == 0, w[:, n - half :], w[:, :half])

    own = jnp.concatenate([query_weight, key_weight, value_matrix], axis=1)
    edge = jnp.concatenate(
        [edge_of(query_weight), edge_of(key_weight), edge_of(value_matrix)], axis=1
    )
    gains = jnp.stack([attn_gain, ffn_gain])
    h_s, edge_s, gain_s, own_s, gate_s, up_s, down_s = exchange(
        ("all", "all", "row", "row", "cols", "cols", "lead"),
        [
            hidden_in,
            edge,
            gains,
            own,
            gate_weight,
            up_weight,
            down_weight.reshape(2, fw, down_weight.shape[1]),
        ],
        1,
    )
    output_weight, out_grad, h_s = lax.optimization_barrier((output_weight, out_grad, h_s))
    wo_x = lax.ppermute(output_weight, "col", PAIR)
    og_x = lax.ppermute(out_grad, "col", PAIR)
    gains = jnp.transpose(gain_s, (1, 0, 2)).reshape(2, width)
    g_one, g_two = gains[0:1], gains[1:2]
    hid = flat(h_s)
    resid = hid.astype(F32)

    frequency = rope_base ** (
        -(jnp.arange(HEAD_SIZE // 2, dtype=F32) * 2.0) / HEAD_SIZE
    )
    angles = position_ids.astype(F32)[:, None] * frequency[None, :]
    cos, sin = jnp.cos(angles), jnp.sin(angles)
    cos = jnp.concatenate([cos, cos], axis=1)
    sin = jnp.concatenate([sin, sin], axis=1)

    own = own_s.reshape(width, qc + 2 * kc)
    edge_x = lax.dynamic_index_in_dim(edge_s, 1 - c, 0, keepdims=False).reshape(width, 3 * half)

    def local(lo, n, e, size):
        ext = ordered(c, own[:, lo : lo + n], edge_x[:, e * half : (e + 1) * half], 1)
        step = (ext.shape[1] - size)
        return lax.dynamic_slice_in_dim(ext, r * step, size, 1)

    wq = local(0, qc, 0, slots_q)
    wk = local(qc, kc, 1, slots_k)
    wv = local(qc + kc, kc, 2, slots_k)
    w_three = jnp.concatenate([wq, wk, wv], axis=1)
    w_all = jnp.concatenate([w_three, swap_halves(wq), swap_halves(wk)], axis=1)
    inv_one = lax.rsqrt(jnp.mean(resid * resid, axis=1, keepdims=True) + epsilon)
    normed_one = (resid * inv_one * g_one).astype(BF16)
    proj = matmul(normed_one, w_all).astype(BF16)
    e1, e2, e3, e4 = slots_q, slots_q + slots_k, slots_q + 2 * slots_k, 2 * slots_q + 2 * slots_k
    q, k, v, qp, kp = proj[:, :e1], proj[:, e1:e2], proj[:, e2:e3], proj[:, e3:e4], proj[:, e4:]
    heads = slots_q // HEAD_SIZE
    group = QUERY_HEADS // KEY_VALUE_HEADS
    first = c * (QUERY_HEADS - 2 * heads) + r * heads
    sel = (first + jnp.arange(heads, dtype=jnp.int32)) // group - first // group
    seg_col, seg_row = segment_ids[:, None], segment_ids[None, :]
    att, lt, qr, qrp, kr, krp = attn_forward(q, k, v, qp, kp, cos, sin, seg_col, seg_row, sel)

    pair_wo = jnp.stack([output_weight, wo_x])
    pair_og = jnp.stack([out_grad, og_x])
    att_s, wo_s, og_s = exchange(("all", "row", "row"), [att, pair_wo, pair_og], 2)
    def cols_first(s):
        s = jnp.where(c == 0, s, s[:, ::-1])
        return jnp.transpose(s, (1, 0, 2, 3))

    wo = flat(cols_first(wo_s))
    og = flat(cols_first(og_s))
    att_all = jnp.transpose(att_s.reshape(4, t, slots_q), (1, 0, 2)).reshape(t, 4 * slots_q)
    wo_pad = jnp.concatenate(
        [wo[: 2 * slots_q], jnp.zeros((HEAD_SIZE, width), BF16), wo[2 * slots_q :]], axis=0
    )
    mid = resid + matmul(att_all, wo_pad)
    inv_two = lax.rsqrt(jnp.mean(mid * mid, axis=1, keepdims=True) + epsilon)
    normed_two = (mid * inv_two * g_two).astype(BF16)
    gate_w = gate_s.reshape(width, fw)
    up_w = up_s.reshape(width, fw)
    gate = matmul(normed_two, gate_w)
    up = matmul(normed_two, up_w)
    sig = jax.nn.sigmoid(gate)
    silu = gate * sig
    inner = (silu * up).astype(BF16)
    down_w = jnp.transpose(down_s, (1, 0, 2)).reshape(fw, width)
    inner_grad = contract_cols(og, down_w)
    gate_grad = (inner_grad * up * sig * (1.0 + gate * (1.0 - sig))).astype(BF16)
    up_grad = (inner_grad * silu).astype(BF16)
    both = jnp.concatenate([gate_grad, up_grad], axis=1)
    both_w = jnp.concatenate([gate_w, up_w], axis=1)
    part_two = contract_cols(both, both_w).astype(BF16).reshape(2, 2, t // 4, width)

    slot = 2 * c + r
    def quarter(x):
        return lax.dynamic_slice_in_dim(x, slot * (t // 4), t // 4, 0)

    mg, mg_s, gg_two = mid_back(part_two, quarter(mid), quarter(og), g_two, 3)
    mg_all = mg_s.reshape(t, width)
    wo_mine = lax.dynamic_slice_in_dim(wo_pad, slot * slots_q, slots_q, 0)
    da = contract_cols(mg_all, wo_mine).astype(BF16)
    pg = attn_backward(qr, qrp, kr, krp, v, lt, att, da, cos, sin, seg_col, seg_row, sel)
    part_one = contract_cols(pg, w_three).astype(BF16).reshape(2, 2, t // 4, width)
    in_grad, gg_one = in_back(part_one, quarter(hid), mg, g_one, 4)
    hidden_in_grad = in_grad.reshape(t // 2, width // 2)

    def row_half(x):
        return lax.dynamic_slice_in_dim(x, r * (width // 2), width // 2, 1)

    hand = jnp.concatenate([both, inner], axis=1)
    hand_x = lax.ppermute(hand, "row", PAIR)
    gate_full = ordered(r, hand[:, :fw], hand_x[:, :fw], 1)
    up_full = ordered(r, hand[:, fw : 2 * fw], hand_x[:, fw : 2 * fw], 1)
    inner_full = ordered(r, hand[:, 2 * fw :], hand_x[:, 2 * fw :], 1)
    n2 = row_half(normed_two)
    gate_wg = contract_rows(n2, gate_full).astype(BF16)
    up_wg = contract_rows(n2, up_full).astype(BF16)
    down_wg = contract_rows(inner_full, row_half(og)).astype(BF16)
    down_t = lax.psum_scatter(down_wg[None], "dp", scatter_dimension=1, tiled=True).astype(F32)
    gate_t = lax.psum_scatter(gate_wg[None], "dp", scatter_dimension=2, tiled=True).astype(F32)
    up_t = lax.psum_scatter(up_wg[None], "dp", scatter_dimension=2, tiled=True).astype(F32)

    part_out = jnp.stack(
        [matmul(inner, down_s[0]).astype(BF16), matmul(inner, down_s[1]).astype(BF16)]
    ).reshape(2, 2, t // 2, width // 2)
    part_out = jnp.transpose(part_out, (1, 0, 2, 3))
    my_mid = lax.dynamic_slice(mid, (c * (t // 2), r * (width // 2)), (t // 2, width // 2))
    hidden_out = reduce_out(part_out, my_mid, 5)

    att15 = jnp.concatenate(
        [att_all[:, : 2 * slots_q], att_all[:, 2 * slots_q + HEAD_SIZE :]], axis=1
    )
    att_c = lax.dynamic_slice_in_dim(att15, c * qc, qc, 1)
    out_wg = contract_rows(att_c, row_half(mg_all))
    pg_x = lax.ppermute(pg, "row", PAIR)
    pg0 = jnp.where(r == 0, pg, pg_x).astype(F32)
    pg1 = jnp.where(r == 0, pg_x, pg).astype(F32)
    ext_q = jnp.concatenate([pg0[:, :e1], pg1[:, :e1]], axis=1)

    def ext_of(lo):
        z = jnp.zeros((t, HEAD_SIZE), F32)
        a, b = pg0[:, lo : lo + slots_k], pg1[:, lo : lo + slots_k]
        return jnp.concatenate([a, z], axis=1) + jnp.concatenate([z, b], axis=1)

    exts = [ext_q, ext_of(e1), ext_of(e2)]
    sends = [jnp.where(c == 0, x[:, -half:], x[:, :half]) for x in exts]
    got = lax.ppermute(jnp.concatenate(sends, axis=1).astype(BF16), "col", PAIR).astype(F32)
    finals = []
    for i, x in enumerate(exts):
        n = x.shape[1]
        g = got[:, i * half : (i + 1) * half]
        low = jnp.concatenate([x[:, : n - 2 * half], x[:, n - 2 * half : n - half] + g], axis=1)
        high = jnp.concatenate([x[:, half : 2 * half] + g, x[:, 2 * half :]], axis=1)
        finals.append(jnp.where(c == 0, low, high).astype(BF16))
    proj_wg = contract_rows(row_half(normed_one), jnp.concatenate(finals, axis=1))
    proj_t, out_t = lax.psum((proj_wg.astype(BF16), out_wg.astype(BF16)), "dp")
    gain_t = lax.psum(jnp.concatenate([gg_one, gg_two], axis=0), ("dp", "row", "col"))
    gain_t = row_half(gain_t)
    proj_t = proj_t.astype(F32)
    return (
        hidden_out,
        hidden_in_grad,
        gain_t[0],
        proj_t[:, :qc],
        proj_t[:, qc : qc + kc],
        proj_t[:, qc + kc :],
        out_t.astype(F32),
        gain_t[1],
        gate_t,
        up_t,
        down_t,
    )


def solution(mesh):
    return jax.shard_map(
        on_device,
        mesh=mesh,
        in_specs=(
            P(("dp", "col"), "row"),
            P("dp"),
            P("dp"),
            P("row"),
            P("row", "col"),
            P("row", "col"),
            P("row", "col"),
            P("col", "row"),
            P("row"),
            P("row", "col"),
            P("row", "col"),
            P("col", "row"),
            P(("dp", "col"), "row"),
        ),
        out_specs=(
            P(("dp", "col"), "row"),
            P(("dp", "col"), "row"),
            P("row"),
            P("row", "col"),
            P("row", "col"),
            P("row", "col"),
            P("col", "row"),
            P("row"),
            P("col", "row", "dp"),
            P("col", "row", "dp"),
            P("col", "dp", "row"),
        ),
        check_vma=False,
    )
```

```python
import functools

import jax
import jax.numpy as jnp
from jax import lax
from jax.experimental import pallas as pl
from jax.experimental.pallas import tpu as pltpu
from jax.sharding import PartitionSpec as P

HEAD_SIZE = 64
QUERY_HEADS = 15
KEY_VALUE_HEADS = 5
epsilon = 1e-05
rope_base = 10000.0
masked_score = -1e30
MESH = pl.DeviceIdType.MESH
F32 = jnp.float32
BF16 = jnp.bfloat16
VM = pl.BlockSpec(memory_space=pltpu.VMEM)


def matmul(left, right):
    return jnp.dot(left, right, preferred_element_type=F32)


def contract_rows(left, right):
    return lax.dot_general(left, right, (((0,), (0,)), ((), ())), preferred_element_type=F32)


def contract_cols(left, right):
    return lax.dot_general(left, right, (((1,), (1,)), ((), ())), preferred_element_type=F32)


def greet(axes):
    barrier = pltpu.get_barrier_semaphore()
    for axis in axes:
        other = 1 - lax.axis_index(axis)
        pl.semaphore_signal(barrier, inc=1, device_id={axis: other}, device_id_type=MESH)
    pl.semaphore_wait(barrier, len(axes))


def remote(src, dst, send_sem, recv_sem, axis):
    return pltpu.make_async_remote_copy(
        src_ref=src,
        dst_ref=dst,
        send_sem=send_sem,
        recv_sem=recv_sem,
        device_id={axis: 1 - lax.axis_index(axis)},
        device_id_type=MESH,
    )


def call(body, outs, scratch, args, cid, vmem=60 * 2**20):
    return pl.pallas_call(
        body,
        out_shape=outs,
        in_specs=[VM] * len(args),
        out_specs=[VM] * len(outs),
        scratch_shapes=scratch,
        compiler_params=pltpu.CompilerParams(
            collective_id=cid, has_side_effects=cid is not None, vmem_limit_bytes=vmem
        ),
    )(*args)


def exchange(kinds, arrays, cid):
    n = len(arrays)

    def body(*refs):
        ins, outs, sems = refs[:n], refs[n : 2 * n], refs[2 * n]
        r, c = lax.axis_index("row"), lax.axis_index("col")
        greet(("row", "col") if "all" in kinds else ("row",))
        pending, firsts = [], []
        for i, kind in enumerate(kinds):
            if kind == "all":
                cp = remote(ins[i], outs[i].at[c, r], sems.at[i, 0], sems.at[i, 1], "col")
                cp.start()
                firsts.append((i, cp))
        for i, kind in enumerate(kinds):
            if kind == "all":
                src, keep, dst = ins[i], ins[i], outs[i].at[c, r]
            elif kind == "row":
                src, keep, dst = ins[i], ins[i], outs[i].at[r]
            elif kind == "lead":
                src, keep, dst = ins[i].at[1 - r], ins[i].at[r], outs[i].at[r]
            else:
                w = ins[i].shape[1] // 2
                src = ins[i].at[:, pl.ds(pl.multiple_of((1 - r) * w, 128), w)]
                keep = ins[i].at[:, pl.ds(pl.multiple_of(r * w, 128), w)]
                dst = outs[i].at[r]
            cp = remote(src, dst, sems.at[i, 2], sems.at[i, 3], "row")
            cp.start()
            loc = pltpu.make_async_copy(keep, dst, sems.at[i, 6])
            loc.start()
            pending += [cp, loc]
        for i, cp in firsts:
            cp.wait_recv()
            fw = remote(
                outs[i].at[1 - c, r], outs[i].at[1 - c, r], sems.at[i, 4], sems.at[i, 5], "row"
            )
            fw.start()
            pending.append(fw)
        for _, cp in firsts:
            cp.wait_send()
        for cp in pending:
            cp.wait()

    outs = []
    for kind, a in zip(kinds, arrays):
        if kind == "all":
            s = (2, 2) + a.shape
        elif kind == "row":
            s = (2,) + a.shape
        elif kind == "lead":
            s = a.shape
        else:
            s = (2, a.shape[0], a.shape[1] // 2)
        outs.append(jax.ShapeDtypeStruct(s, a.dtype))
    return call(body, outs, [pltpu.SemaphoreType.DMA((n, 7))], arrays, cid)


def scatter_scratch(part):
    s, d = part.shape[2:], part.dtype
    return [
        pltpu.VMEM((2,) + s, d),
        pltpu.VMEM(s, d),
        pltpu.VMEM(s, d),
        pltpu.SemaphoreType.DMA((6,)),
    ]


def scatter_sum(part, land, out_x, land_x, sems):
    r, c = lax.axis_index("row"), lax.axis_index("col")
    first = remote(part.at[1 - c, 1 - r], land.at[0], sems.at[0], sems.at[1], "row")
    second = remote(part.at[c, 1 - r], land.at[1], sems.at[2], sems.at[3], "row")
    first.start()
    second.start()
    first.wait_recv()
    out_x[...] = (part[1 - c, r].astype(F32) + land[0].astype(F32)).astype(out_x.dtype)
    third = remote(out_x, land_x, sems.at[4], sems.at[5], "col")
    third.start()
    second.wait_recv()
    mine = part[c, r].astype(F32) + land[1].astype(F32)
    third.wait_recv()
    total = mine + land_x[...].astype(F32)

    def finish():
        first.wait_send()
        second.wait_send()
        third.wait_send()

    return total, finish


def reduce_out(part, resid, cid):
    def body(part, resid, out, land, out_x, land_x, sems):
        greet(("row", "col"))
        total, finish = scatter_sum(part, land, out_x, land_x, sems)
        out[...] = (total + resid[...]).astype(BF16)
        finish()

    outs = [jax.ShapeDtypeStruct(resid.shape, BF16)]
    return call(body, outs, scatter_scratch(part), [part, resid], cid)[0]


def norm_back(grad, resid, gain):
    width = resid.shape[1]
    inv = lax.rsqrt(jnp.sum(resid * resid, axis=1, keepdims=True) / width + epsilon)
    unit = resid * inv
    weighted = grad * gain
    mean = jnp.sum(weighted * unit, axis=1, keepdims=True) / width
    return inv * (weighted - unit * mean), jnp.sum(grad * unit, axis=0, keepdims=True)


def mid_back(part, mid, og, gain, cid):
    def body(part, mid, og, gain, mg, mg_all, gg, land, out_x, land_x, sems, sems2):
        r, c = lax.axis_index("row"), lax.axis_index("col")
        greet(("row", "col"))
        total, finish = scatter_sum(part, land, out_x, land_x, sems)
        back, gsum = norm_back(total, mid[...], gain[...])
        back = back + og[...].astype(F32)
        mg_all[c, r] = back.astype(BF16)
        mine = mg_all.at[c, r]
        a = remote(mine, mine, sems2.at[0], sems2.at[1], "col")
        b = remote(mine, mine, sems2.at[2], sems2.at[3], "row")
        a.start()
        b.start()
        mg[...] = back
        gg[...] = gsum
        a.wait_recv()
        theirs = mg_all.at[1 - c, r]
        f = remote(theirs, theirs, sems2.at[4], sems2.at[5], "row")
        f.start()
        a.wait_send()
        b.wait()
        f.wait()
        finish()

    t, w = mid.shape
    outs = [
        jax.ShapeDtypeStruct((t, w), F32),
        jax.ShapeDtypeStruct((2, 2, t, w), BF16),
        jax.ShapeDtypeStruct((1, w), F32),
    ]
    scratch = scatter_scratch(part) + [pltpu.SemaphoreType.DMA((6,))]
    return call(body, outs, scratch, [part, mid, og, gain], cid)


def in_back(part, hid, mg, gain, cid):
    def body(part, hid, mg, gain, out, gg, land, out_x, land_x, sems, swap, got, sems2):
        r, c = lax.axis_index("row"), lax.axis_index("col")
        greet(("row", "col"))
        total, finish = scatter_sum(part, land, out_x, land_x, sems)
        back, gsum = norm_back(total, hid[...].astype(F32), gain[...])
        back = back + mg[...]
        w = back.shape[1] // 2
        swap[0] = back[:, :w]
        swap[1] = back[:, w:]
        a = remote(swap.at[1 - r], got, sems2.at[0], sems2.at[1], "row")
        a.start()
        gg[...] = gsum
        out[r] = swap[r]
        a.wait()
        out[1 - r] = got[...]
        finish()

    t, w = hid.shape
    outs = [jax.ShapeDtypeStruct((2, t, w // 2), F32), jax.ShapeDtypeStruct((1, w), F32)]
    scratch = scatter_scratch(part) + [
        pltpu.VMEM((2, t, w // 2), F32),
        pltpu.VMEM((t, w // 2), F32),
        pltpu.SemaphoreType.DMA((2,)),
    ]
    return call(body, outs, scratch, [part, hid, mg, gain], cid)


def dp_reduce(arrays, gains, cid):
    m = len(arrays)
    n, t, w = arrays[0].shape
    hop = 2
    far = n // hop

    def body(*refs):
        g, gain = refs[:m], refs[m]
        every, outs, gsum = refs[m + 1], refs[m + 2 : 2 * m + 1], refs[2 * m + 1]
        land, summed, got, g_mine, g_land, ys, zs, ags, gs = refs[2 * m + 2 :]
        me = lax.axis_index("dp")
        hi, lo = me // hop, me % hop
        near = hi * hop + 1 - lo
        at = [lax.rem(hi + k, far) for k in range(far)]
        back = [lax.rem(hi + far - k, far) for k in range(far)]

        def to(src, dst, send, recv, dev):
            return pltpu.make_async_remote_copy(
                src_ref=src, dst_ref=dst, send_sem=send, recv_sem=recv,
                device_id=dev, device_id_type=MESH,
            )

        barrier = pltpu.get_barrier_semaphore()
        peers = [{"dp": near}] + [{"dp": at[k] * hop + lo} for k in range(1, far)]
        peers += [{a: 1 - lax.axis_index(a)} for a in ("row", "col")]
        for dev in peers:
            pl.semaphore_signal(barrier, inc=1, device_id=dev, device_id_type=MESH)
        pl.semaphore_wait(barrier, len(peers))

        ending = []
        g_mine[0] = gain[...]
        gy = to(g_mine.at[0], g_land.at[0], gs.at[0, 0], gs.at[1, 0], {"dp": near})
        gy.start()
        order = list(range(1, far)) + [0]
        ycopy, zcopy = {}, {}
        for i in range(m):
            for k in order:
                cp = to(
                    g[i].at[at[k] * hop + 1 - lo], land.at[i, k],
                    ys.at[0, i, k], ys.at[1, i, k], {"dp": near},
                )
                cp.start()
                ycopy[i, k] = cp
        gy.wait()
        g_mine[1] = g_mine[0] + g_land[0]
        gz = []
        for k in range(1, far):
            cp = to(
                g_mine.at[1], g_land.at[k], gs.at[0, k], gs.at[1, k], {"dp": at[k] * hop + lo}
            )
            cp.start()
            gz.append(cp)

        def pair_sum(i):
            for k in order:
                ycopy[i, k].wait_recv()
                if k:
                    mine = g[i][at[k] * hop + lo].astype(F32)
                    summed[i, k] = (mine + land[i, k].astype(F32)).astype(BF16)
                    cp = to(
                        summed.at[i, k], got.at[i, k],
                        zs.at[0, i, k], zs.at[1, i, k], {"dp": at[k] * hop + lo},
                    )
                    cp.start()
                    zcopy[i, k] = cp

        def total(i):
            acc = g[i][me].astype(F32) + land[i, 0].astype(F32)
            for k in range(1, far):
                zcopy[i, k].wait_recv()
                acc += got[i, k].astype(F32)
            return acc

        spread = []

        def send_all():
            every[me] = total(0).astype(BF16)
            mine = every.at[me]
            cp = to(mine, mine, ags.at[0, 0], ags.at[1, 0], {"dp": near})
            cp.start()
            spread.append(cp)
            for k in range(1, far):
                cp = to(mine, mine, ags.at[2, k], ags.at[3, k], {"dp": at[k] * hop + lo})
                cp.start()
                spread.append(cp)

        pair_sum(0)
        if m > 1:
            pair_sum(1)
        send_all()
        for i in range(2, m):
            pair_sum(i)
        for k in range(1, far):
            spread[k].wait_recv()
            came = every.at[back[k] * hop + lo]
            cp = to(came, came, ags.at[0, k], ags.at[1, k], {"dp": near})
            cp.start()
            ending.append(cp)
        for cp in gz:
            cp.wait()
        acc = g_mine[1]
        for k in range(1, far):
            acc += g_land[k]
        for j, axis in enumerate(("col", "row")):
            g_mine[2 + j] = acc
            cp = to(
                g_mine.at[2 + j], g_land.at[far + j], gs.at[0, far + j], gs.at[1, far + j],
                {axis: 1 - lax.axis_index(axis)},
            )
            cp.start()
            cp.wait()
            acc = acc + g_land[far + j]
        gsum[...] = acc
        for i in range(1, m):
            outs[i - 1][...] = total(i)
        spread[0].wait()
        for cp in spread[1:]:
            cp.wait_send()
        for cp in ending:
            cp.wait()
        for cp in ycopy.values():
            cp.wait_send()
        for cp in zcopy.values():
            cp.wait_send()

    outs = [jax.ShapeDtypeStruct((n, t, w), BF16)]
    outs += [jax.ShapeDtypeStruct((t, w), F32)] * (m - 1)
    outs += [jax.ShapeDtypeStruct(gains.shape, F32)]
    dma = pltpu.SemaphoreType.DMA
    block = pltpu.VMEM((m, far, t, w), BF16)
    scratch = [
        block, block, block,
        pltpu.VMEM((4,) + gains.shape, F32),
        pltpu.VMEM((far + 2,) + gains.shape, F32),
        dma((2, m, far)), dma((2, m, far)), dma((4, far)), dma((2, far + 2)),
    ]
    return call(body, outs, scratch, list(arrays) + [gains], cid)


def head(values, h):
    return values[:, h * HEAD_SIZE : (h + 1) * HEAD_SIZE]


def turn(x, xp, cos, sin):
    x, xp = x.astype(F32), xp.astype(F32)
    return (x * cos + xp * sin).astype(BF16), (xp * cos - x * sin).astype(BF16)


def pick(flag, a, b):
    return jnp.where(flag, b, a)


def attn_forward(q, k, v, qp, kp, cos, sin, seg_col, seg_row, sel):
    heads = q.shape[1] // HEAD_SIZE
    t = q.shape[0]

    def body(sel, q, k, v, qp, kp, cos, sin, seg_c, seg_r, out, lt, qr, qrp, kr, krp):
        co, si = cos[...], sin[...]
        at = lax.broadcasted_iota(jnp.int32, (t, t), 0)
        to = lax.broadcasted_iota(jnp.int32, (t, t), 1)
        allowed = (seg_c[...] == seg_r[...]) & (to <= at)
        kk = []
        for g in range(2):
            a, b = turn(head(k, g), head(kp, g), co, si)
            kr[:, g * HEAD_SIZE : (g + 1) * HEAD_SIZE] = a
            krp[:, g * HEAD_SIZE : (g + 1) * HEAD_SIZE] = b
            kk.append(a)
        vv = [head(v, 0), head(v, 1)]
        for h in range(heads):
            a, b = turn(head(q, h), head(qp, h), co, si)
            qr[:, h * HEAD_SIZE : (h + 1) * HEAD_SIZE] = a
            qrp[:, h * HEAD_SIZE : (h + 1) * HEAD_SIZE] = b
            f = sel[h] == 1
            s = contract_cols(a, pick(f, *kk)) * HEAD_SIZE**-0.5
            s = jnp.where(allowed, s, masked_score)
            m = jnp.max(s, axis=1, keepdims=True)
            l = m + jnp.log(jnp.sum(jnp.exp(s - m), axis=1, keepdims=True))
            lt[:, h : h + 1] = l
            p = jnp.exp(s - l).astype(BF16)
            out[:, h * HEAD_SIZE : (h + 1) * HEAD_SIZE] = matmul(p, pick(f, *vv)).astype(BF16)

    outs = [
        jax.ShapeDtypeStruct(q.shape, BF16),
        jax.ShapeDtypeStruct((t, heads), F32),
        jax.ShapeDtypeStruct(q.shape, BF16),
        jax.ShapeDtypeStruct(q.shape, BF16),
        jax.ShapeDtypeStruct(k.shape, BF16),
        jax.ShapeDtypeStruct(k.shape, BF16),
    ]
    return pl.pallas_call(
        body,
        out_shape=outs,
        in_specs=[pl.BlockSpec(memory_space=pltpu.SMEM)] + [VM] * 9,
        out_specs=[VM] * 6,
        compiler_params=pltpu.CompilerParams(vmem_limit_bytes=60 * 2**20),
        name="attn_forward",
    )(sel, q, k, v, qp, kp, cos, sin, seg_col, seg_row)


def attn_backward(qr, qrp, kr, krp, v, lt, att, da, cos, sin, seg_col, seg_row, sel):
    heads = qr.shape[1] // HEAD_SIZE
    t = qr.shape[0]
    kw = kr.shape[1]

    def body(sel, qr, qrp, kr, krp, v, lt, att, da, cos, sin, seg_c, seg_r, out):
        co, si = cos[...], sin[...]
        at = lax.broadcasted_iota(jnp.int32, (t, t), 0)
        to = lax.broadcasted_iota(jnp.int32, (t, t), 1)
        allowed = (seg_c[...] == seg_r[...]) & (to <= at)
        kk = [jnp.concatenate([head(kr, g), head(krp, g)], axis=1) for g in range(2)]
        vv = [head(v, 0), head(v, 1)]
        dk = [jnp.zeros((t, 2 * HEAD_SIZE), F32)] * 2
        dv = [jnp.zeros((t, HEAD_SIZE), F32)] * 2
        for h in range(heads):
            f = sel[h] == 1
            kc = pick(f, *kk)
            vh = pick(f, *vv)
            qh = head(qr, h)
            dh = head(da, h)
            s = contract_cols(qh, kc[:, :HEAD_SIZE]) * HEAD_SIZE**-0.5
            s = jnp.where(allowed, s, masked_score)
            p = jnp.exp(s - lt[:, h : h + 1])
            dot = jnp.sum(dh.astype(F32) * head(att, h).astype(F32), axis=1, keepdims=True)
            dvh = contract_rows(p.astype(BF16), dh)
            dp = contract_cols(dh, vh)
            ds = (p * (dp - dot) * HEAD_SIZE**-0.5).astype(BF16)
            dq = matmul(ds, kc)
            dq = dq[:, :HEAD_SIZE] * co - dq[:, HEAD_SIZE:] * si
            out[:, h * HEAD_SIZE : (h + 1) * HEAD_SIZE] = dq.astype(BF16)
            dkh = contract_rows(ds, jnp.concatenate([qh, head(qrp, h)], axis=1))
            zk, zv = jnp.zeros_like(dkh), jnp.zeros_like(dvh)
            dk = [dk[0] + pick(f, dkh, zk), dk[1] + pick(f, zk, dkh)]
            dv = [dv[0] + pick(f, dvh, zv), dv[1] + pick(f, zv, dvh)]
        base = heads * HEAD_SIZE
        for g in range(2):
            lo = base + g * HEAD_SIZE
            back = dk[g][:, :HEAD_SIZE] * co - dk[g][:, HEAD_SIZE:] * si
            out[:, lo : lo + HEAD_SIZE] = back.astype(BF16)
            out[:, lo + kw : lo + kw + HEAD_SIZE] = dv[g].astype(BF16)

    return pl.pallas_call(
        body,
        out_shape=jax.ShapeDtypeStruct((t, heads * HEAD_SIZE + 2 * kw), BF16),
        in_specs=[pl.BlockSpec(memory_space=pltpu.SMEM)] + [VM] * 12,
        out_specs=VM,
        compiler_params=pltpu.CompilerParams(vmem_limit_bytes=60 * 2**20),
        name="attn_backward",
    )(sel, qr, qrp, kr, krp, v, lt, att, da, cos, sin, seg_col, seg_row)


def swap_halves(weights):
    w = weights.reshape(weights.shape[0], -1, 2, HEAD_SIZE // 2)
    return jnp.concatenate([-w[:, :, 1:], w[:, :, :1]], axis=2).reshape(weights.shape)


def flat(slots):
    a, b, t, w = slots.shape
    return jnp.transpose(slots, (0, 2, 1, 3)).reshape(a * t, b * w)


def ordered(r, mine, theirs, axis):
    return jnp.where(
        r == 0,
        jnp.concatenate([mine, theirs], axis=axis),
        jnp.concatenate([theirs, mine], axis=axis),
    )


PAIR = [(0, 1), (1, 0)]


def on_device(
    hidden_in,
    segment_ids,
    position_ids,
    attn_gain,
    query_weight,
    key_weight,
    value_matrix,
    output_weight,
    ffn_gain,
    gate_weight,
    up_weight,
    down_weight,
    out_grad,
):
    r, c = lax.axis_index("row"), lax.axis_index("col")
    t = segment_ids.shape[0]
    width = 2 * hidden_in.shape[1]
    qc, kc = query_weight.shape[1], key_weight.shape[1]
    half = qc % HEAD_SIZE
    fw = gate_weight.shape[1] // 2
    slots_q = (qc + half) // 2
    slots_k = 2 * HEAD_SIZE

    def edge_of(w):
        n = w.shape[1]
        return jnp.where(c == 0, w[:, n - half :], w[:, :half])

    own = jnp.concatenate([query_weight, key_weight, value_matrix], axis=1)
    edge = jnp.concatenate(
        [edge_of(query_weight), edge_of(key_weight), edge_of(value_matrix)], axis=1
    )
    gains = jnp.stack([attn_gain, ffn_gain])
    h_s, edge_s, gain_s, own_s, gate_s, up_s, down_s = exchange(
        ("all", "all", "row", "row", "cols", "cols", "lead"),
        [
            hidden_in,
            edge,
            gains,
            own,
            gate_weight,
            up_weight,
            down_weight.reshape(2, fw, down_weight.shape[1]),
        ],
        1,
    )
    output_weight, out_grad, h_s = lax.optimization_barrier((output_weight, out_grad, h_s))
    wo_x = lax.ppermute(output_weight, "col", PAIR)
    og_x = lax.ppermute(out_grad, "col", PAIR)
    gains = jnp.transpose(gain_s, (1, 0, 2)).reshape(2, width)
    g_one, g_two = gains[0:1], gains[1:2]
    hid = flat(h_s)
    resid = hid.astype(F32)

    frequency = rope_base ** (
        -(jnp.arange(HEAD_SIZE // 2, dtype=F32) * 2.0) / HEAD_SIZE
    )
    angles = position_ids.astype(F32)[:, None] * frequency[None, :]
    cos, sin = jnp.cos(angles), jnp.sin(angles)
    cos = jnp.concatenate([cos, cos], axis=1)
    sin = jnp.concatenate([sin, sin], axis=1)

    own = own_s.reshape(width, qc + 2 * kc)
    edge_x = lax.dynamic_index_in_dim(edge_s, 1 - c, 0, keepdims=False).reshape(width, 3 * half)

    def local(lo, n, e, size):
        ext = ordered(c, own[:, lo : lo + n], edge_x[:, e * half : (e + 1) * half], 1)
        step = (ext.shape[1] - size)
        return lax.dynamic_slice_in_dim(ext, r * step, size, 1)

    wq = local(0, qc, 0, slots_q)
    wk = local(qc, kc, 1, slots_k)
    wv = local(qc + kc, kc, 2, slots_k)
    w_three = jnp.concatenate([wq, wk, wv], axis=1)
    w_all = jnp.concatenate([w_three, swap_halves(wq), swap_halves(wk)], axis=1)
    inv_one = lax.rsqrt(jnp.mean(resid * resid, axis=1, keepdims=True) + epsilon)
    normed_one = (resid * inv_one * g_one).astype(BF16)
    proj = matmul(normed_one, w_all).astype(BF16)
    e1, e2, e3, e4 = slots_q, slots_q + slots_k, slots_q + 2 * slots_k, 2 * slots_q + 2 * slots_k
    q, k, v, qp, kp = proj[:, :e1], proj[:, e1:e2], proj[:, e2:e3], proj[:, e3:e4], proj[:, e4:]
    heads = slots_q // HEAD_SIZE
    group = QUERY_HEADS // KEY_VALUE_HEADS
    first = c * (QUERY_HEADS - 2 * heads) + r * heads
    sel = (first + jnp.arange(heads, dtype=jnp.int32)) // group - first // group
    seg_col, seg_row = segment_ids[:, None], segment_ids[None, :]
    att, lt, qr, qrp, kr, krp = attn_forward(q, k, v, qp, kp, cos, sin, seg_col, seg_row, sel)

    pair_wo = jnp.stack([output_weight, wo_x])
    pair_og = jnp.stack([out_grad, og_x])
    att_s, wo_s, og_s = exchange(("all", "row", "row"), [att, pair_wo, pair_og], 2)
    def cols_first(s):
        s = jnp.where(c == 0, s, s[:, ::-1])
        return jnp.transpose(s, (1, 0, 2, 3))

    wo = flat(cols_first(wo_s))
    og = flat(cols_first(og_s))
    att_all = jnp.transpose(att_s.reshape(4, t, slots_q), (1, 0, 2)).reshape(t, 4 * slots_q)
    wo_pad = jnp.concatenate(
        [wo[: 2 * slots_q], jnp.zeros((HEAD_SIZE, width), BF16), wo[2 * slots_q :]], axis=0
    )
    mid = resid + matmul(att_all, wo_pad)
    inv_two = lax.rsqrt(jnp.mean(mid * mid, axis=1, keepdims=True) + epsilon)
    normed_two = (mid * inv_two * g_two).astype(BF16)
    gate_w = gate_s.reshape(width, fw)
    up_w = up_s.reshape(width, fw)
    gate = matmul(normed_two, gate_w)
    up = matmul(normed_two, up_w)
    sig = jax.nn.sigmoid(gate)
    silu = gate * sig
    inner = (silu * up).astype(BF16)
    down_w = jnp.transpose(down_s, (1, 0, 2)).reshape(fw, width)
    inner_grad = contract_cols(og, down_w)
    gate_grad = (inner_grad * up * sig * (1.0 + gate * (1.0 - sig))).astype(BF16)
    up_grad = (inner_grad * silu).astype(BF16)
    both = jnp.concatenate([gate_grad, up_grad], axis=1)
    both_w = jnp.concatenate([gate_w, up_w], axis=1)
    part_two = contract_cols(both, both_w).astype(BF16).reshape(2, 2, t // 4, width)

    slot = 2 * c + r
    def quarter(x):
        return lax.dynamic_slice_in_dim(x, slot * (t // 4), t // 4, 0)

    mg, mg_s, gg_two = mid_back(part_two, quarter(mid), quarter(og), g_two, 3)
    mg_all = mg_s.reshape(t, width)
    wo_mine = lax.dynamic_slice_in_dim(wo_pad, slot * slots_q, slots_q, 0)
    da = contract_cols(mg_all, wo_mine).astype(BF16)
    pg = attn_backward(qr, qrp, kr, krp, v, lt, att, da, cos, sin, seg_col, seg_row, sel)
    part_one = contract_cols(pg, w_three).astype(BF16).reshape(2, 2, t // 4, width)
    in_grad, gg_one = in_back(part_one, quarter(hid), mg, g_one, 4)
    hidden_in_grad = in_grad.reshape(t // 2, width // 2)

    def row_half(x):
        return lax.dynamic_slice_in_dim(x, r * (width // 2), width // 2, 1)

    hand = jnp.concatenate([both, inner], axis=1)
    hand_x = lax.ppermute(hand, "row", PAIR)
    gate_full = ordered(r, hand[:, :fw], hand_x[:, :fw], 1)
    up_full = ordered(r, hand[:, fw : 2 * fw], hand_x[:, fw : 2 * fw], 1)
    inner_full = ordered(r, hand[:, 2 * fw :], hand_x[:, 2 * fw :], 1)
    n2 = row_half(normed_two)
    n_dp = lax.axis_size("dp")
    gate_wg = contract_rows(gate_full, n2).astype(BF16)
    up_wg = contract_rows(up_full, n2).astype(BF16)
    down_wg = contract_rows(inner_full, row_half(og)).astype(BF16)

    def blocks(x):
        return x.reshape(n_dp, x.shape[0] // n_dp, x.shape[1])

    part_out = jnp.stack(
        [matmul(inner, down_s[0]).astype(BF16), matmul(inner, down_s[1]).astype(BF16)]
    ).reshape(2, 2, t // 2, width // 2)
    part_out = jnp.transpose(part_out, (1, 0, 2, 3))
    my_mid = lax.dynamic_slice(mid, (c * (t // 2), r * (width // 2)), (t // 2, width // 2))
    hidden_out = reduce_out(part_out, my_mid, 5)

    att15 = jnp.concatenate(
        [att_all[:, : 2 * slots_q], att_all[:, 2 * slots_q + HEAD_SIZE :]], axis=1
    )
    att_c = lax.dynamic_slice_in_dim(att15, c * qc, qc, 1)
    out_wg = contract_rows(att_c, row_half(mg_all))
    pg_x = lax.ppermute(pg, "row", PAIR)
    pg0 = jnp.where(r == 0, pg, pg_x).astype(F32)
    pg1 = jnp.where(r == 0, pg_x, pg).astype(F32)
    ext_q = jnp.concatenate([pg0[:, :e1], pg1[:, :e1]], axis=1)

    def ext_of(lo):
        z = jnp.zeros((t, HEAD_SIZE), F32)
        a, b = pg0[:, lo : lo + slots_k], pg1[:, lo : lo + slots_k]
        return jnp.concatenate([a, z], axis=1) + jnp.concatenate([z, b], axis=1)

    exts = [ext_q, ext_of(e1), ext_of(e2)]
    sends = [jnp.where(c == 0, x[:, -half:], x[:, :half]) for x in exts]
    got = lax.ppermute(jnp.concatenate(sends, axis=1).astype(BF16), "col", PAIR).astype(F32)
    finals = []
    for i, x in enumerate(exts):
        n = x.shape[1]
        g = got[:, i * half : (i + 1) * half]
        low = jnp.concatenate([x[:, : n - 2 * half], x[:, n - 2 * half : n - half] + g], axis=1)
        high = jnp.concatenate([x[:, half : 2 * half] + g, x[:, 2 * half :]], axis=1)
        finals.append(jnp.where(c == 0, low, high).astype(BF16))
    proj_wg = contract_rows(jnp.concatenate(finals, axis=1), row_half(normed_one))
    attn_wg = jnp.concatenate([proj_wg.astype(BF16), out_wg.astype(BF16)], axis=0)
    gain_part = jnp.concatenate([gg_one, gg_two], axis=0)
    attn_t, down_t, gate_t, up_t, gain_t = dp_reduce(
        [blocks(attn_wg), blocks(down_wg), blocks(gate_wg), blocks(up_wg)], gain_part, 6
    )
    gain_t = row_half(gain_t)
    attn_t = attn_t.reshape(attn_wg.shape)
    n_proj = qc + 2 * kc
    proj_t = attn_t[:n_proj].T.astype(F32)
    out_t = attn_t[n_proj:]
    gate_t, up_t, down_t = gate_t.T[None], up_t.T[None], down_t[None]
    return (
        hidden_out,
        hidden_in_grad,
        gain_t[0],
        proj_t[:, :qc],
        proj_t[:, qc : qc + kc],
        proj_t[:, qc + kc :],
        out_t.astype(F32),
        gain_t[1],
        gate_t,
        up_t,
        down_t,
    )


def solution(mesh):
    return jax.shard_map(
        on_device,
        mesh=mesh,
        in_specs=(
            P(("dp", "col"), "row"),
            P("dp"),
            P("dp"),
            P("row"),
            P("row", "col"),
            P("row", "col"),
            P("row", "col"),
            P("col", "row"),
            P("row"),
            P("row", "col"),
            P("row", "col"),
            P("col", "row"),
            P(("dp", "col"), "row"),
        ),
        out_specs=(
            P(("dp", "col"), "row"),
            P(("dp", "col"), "row"),
            P("row"),
            P("row", "col"),
            P("row", "col"),
            P("row", "col"),
            P("col", "row"),
            P("row"),
            P("col", "row", "dp"),
            P("col", "row", "dp"),
            P("col", "dp", "row"),
        ),
        check_vma=False,
    )
```

```python
import functools

import jax
import jax.numpy as jnp
from jax import lax
from jax.experimental import pallas as pl
from jax.experimental.pallas import tpu as pltpu
from jax.sharding import PartitionSpec as P

HEAD_SIZE = 64
QUERY_HEADS = 15
KEY_VALUE_HEADS = 5
epsilon = 1e-05
rope_base = 10000.0
masked_score = -1e30
MESH = pl.DeviceIdType.MESH
F32 = jnp.float32
BF16 = jnp.bfloat16
VM = pl.BlockSpec(memory_space=pltpu.VMEM)


def matmul(left, right):
    return jnp.dot(left, right, preferred_element_type=F32)


def contract_rows(left, right):
    return lax.dot_general(left, right, (((0,), (0,)), ((), ())), preferred_element_type=F32)


def contract_cols(left, right):
    return lax.dot_general(left, right, (((1,), (1,)), ((), ())), preferred_element_type=F32)


def greet(axes):
    barrier = pltpu.get_barrier_semaphore()
    for axis in axes:
        other = 1 - lax.axis_index(axis)
        pl.semaphore_signal(barrier, inc=1, device_id={axis: other}, device_id_type=MESH)
    pl.semaphore_wait(barrier, len(axes))


def remote(src, dst, send_sem, recv_sem, axis):
    return pltpu.make_async_remote_copy(
        src_ref=src,
        dst_ref=dst,
        send_sem=send_sem,
        recv_sem=recv_sem,
        device_id={axis: 1 - lax.axis_index(axis)},
        device_id_type=MESH,
    )


def call(body, outs, scratch, args, cid, vmem=60 * 2**20):
    return pl.pallas_call(
        body,
        out_shape=outs,
        in_specs=[VM] * len(args),
        out_specs=[VM] * len(outs),
        scratch_shapes=scratch,
        compiler_params=pltpu.CompilerParams(
            collective_id=cid, has_side_effects=cid is not None, vmem_limit_bytes=vmem
        ),
    )(*args)


def exchange(kinds, arrays, cid):
    n = len(arrays)

    def body(*refs):
        ins, outs, sems = refs[:n], refs[n : 2 * n], refs[2 * n]
        r, c = lax.axis_index("row"), lax.axis_index("col")
        greet(("row", "col") if "all" in kinds else ("row",))
        pending, firsts = [], []
        for i, kind in enumerate(kinds):
            if kind == "all":
                cp = remote(ins[i], outs[i].at[c, r], sems.at[i, 0], sems.at[i, 1], "col")
                cp.start()
                firsts.append((i, cp))
        for i, kind in enumerate(kinds):
            if kind == "all":
                src, keep, dst = ins[i], ins[i], outs[i].at[c, r]
            elif kind == "row":
                src, keep, dst = ins[i], ins[i], outs[i].at[r]
            elif kind == "lead":
                src, keep, dst = ins[i].at[1 - r], ins[i].at[r], outs[i].at[r]
            else:
                w = ins[i].shape[1] // 2
                src = ins[i].at[:, pl.ds(pl.multiple_of((1 - r) * w, 128), w)]
                keep = ins[i].at[:, pl.ds(pl.multiple_of(r * w, 128), w)]
                dst = outs[i].at[r]
            cp = remote(src, dst, sems.at[i, 2], sems.at[i, 3], "row")
            cp.start()
            loc = pltpu.make_async_copy(keep, dst, sems.at[i, 6])
            loc.start()
            pending += [cp, loc]
        for i, cp in firsts:
            cp.wait_recv()
            fw = remote(
                outs[i].at[1 - c, r], outs[i].at[1 - c, r], sems.at[i, 4], sems.at[i, 5], "row"
            )
            fw.start()
            pending.append(fw)
        for _, cp in firsts:
            cp.wait_send()
        for cp in pending:
            cp.wait()

    outs = []
    for kind, a in zip(kinds, arrays):
        if kind == "all":
            s = (2, 2) + a.shape
        elif kind == "row":
            s = (2,) + a.shape
        elif kind == "lead":
            s = a.shape
        else:
            s = (2, a.shape[0], a.shape[1] // 2)
        outs.append(jax.ShapeDtypeStruct(s, a.dtype))
    return call(body, outs, [pltpu.SemaphoreType.DMA((n, 7))], arrays, cid)


def scatter_scratch(part):
    s, d = part.shape[2:], part.dtype
    return [
        pltpu.VMEM((2,) + s, d),
        pltpu.VMEM(s, d),
        pltpu.VMEM(s, d),
        pltpu.SemaphoreType.DMA((6,)),
    ]


def scatter_sum(part, land, out_x, land_x, sems):
    r, c = lax.axis_index("row"), lax.axis_index("col")
    first = remote(part.at[1 - c, 1 - r], land.at[0], sems.at[0], sems.at[1], "row")
    second = remote(part.at[c, 1 - r], land.at[1], sems.at[2], sems.at[3], "row")
    first.start()
    second.start()
    first.wait_recv()
    out_x[...] = (part[1 - c, r].astype(F32) + land[0].astype(F32)).astype(out_x.dtype)
    third = remote(out_x, land_x, sems.at[4], sems.at[5], "col")
    third.start()
    second.wait_recv()
    mine = part[c, r].astype(F32) + land[1].astype(F32)
    third.wait_recv()
    total = mine + land_x[...].astype(F32)

    def finish():
        first.wait_send()
        second.wait_send()
        third.wait_send()

    return total, finish


def norm_back(grad, resid, gain):
    width = resid.shape[1]
    inv = lax.rsqrt(jnp.sum(resid * resid, axis=1, keepdims=True) / width + epsilon)
    unit = resid * inv
    weighted = grad * gain
    mean = jnp.sum(weighted * unit, axis=1, keepdims=True) / width
    return inv * (weighted - unit * mean), jnp.sum(grad * unit, axis=0, keepdims=True)


def dp_reduce(arrays, gains, cid):
    m = len(arrays)
    n, t, w = arrays[0].shape
    hop = 2
    far = n // hop

    def body(*refs):
        g, gain = refs[:m], refs[m]
        every, outs, gsum = refs[m + 1], refs[m + 2 : 2 * m + 1], refs[2 * m + 1]
        land, summed, got, g_mine, g_land, ys, zs, ags, gs = refs[2 * m + 2 :]
        me = lax.axis_index("dp")
        hi, lo = me // hop, me % hop
        near = hi * hop + 1 - lo
        at = [lax.rem(hi + k, far) for k in range(far)]
        back = [lax.rem(hi + far - k, far) for k in range(far)]

        def to(src, dst, send, recv, dev):
            return pltpu.make_async_remote_copy(
                src_ref=src, dst_ref=dst, send_sem=send, recv_sem=recv,
                device_id=dev, device_id_type=MESH,
            )

        barrier = pltpu.get_barrier_semaphore()
        peers = [{"dp": near}] + [{"dp": at[k] * hop + lo} for k in range(1, far)]
        peers += [{a: 1 - lax.axis_index(a)} for a in ("row", "col")]
        for dev in peers:
            pl.semaphore_signal(barrier, inc=1, device_id=dev, device_id_type=MESH)
        pl.semaphore_wait(barrier, len(peers))

        ending = []
        g_mine[0] = gain[...]
        gy = to(g_mine.at[0], g_land.at[0], gs.at[0, 0], gs.at[1, 0], {"dp": near})
        gy.start()
        order = list(range(1, far)) + [0]
        ycopy, zcopy = {}, {}
        for i in range(m):
            for k in order:
                cp = to(
                    g[i].at[at[k] * hop + 1 - lo], land.at[i, k],
                    ys.at[0, i, k], ys.at[1, i, k], {"dp": near},
                )
                cp.start()
                ycopy[i, k] = cp
        gy.wait()
        g_mine[1] = g_mine[0] + g_land[0]
        gz = []
        for k in range(1, far):
            cp = to(
                g_mine.at[1], g_land.at[k], gs.at[0, k], gs.at[1, k], {"dp": at[k] * hop + lo}
            )
            cp.start()
            gz.append(cp)

        def pair_sum(i):
            for k in order:
                ycopy[i, k].wait_recv()
                if k:
                    mine = g[i][at[k] * hop + lo].astype(F32)
                    summed[i, k] = (mine + land[i, k].astype(F32)).astype(BF16)
                    cp = to(
                        summed.at[i, k], got.at[i, k],
                        zs.at[0, i, k], zs.at[1, i, k], {"dp": at[k] * hop + lo},
                    )
                    cp.start()
                    zcopy[i, k] = cp

        def total(i):
            acc = g[i][me].astype(F32) + land[i, 0].astype(F32)
            for k in range(1, far):
                zcopy[i, k].wait_recv()
                acc += got[i, k].astype(F32)
            return acc

        spread = []

        def send_all():
            every[me] = total(0).astype(BF16)
            mine = every.at[me]
            cp = to(mine, mine, ags.at[0, 0], ags.at[1, 0], {"dp": near})
            cp.start()
            spread.append(cp)
            for k in range(1, far):
                cp = to(mine, mine, ags.at[2, k], ags.at[3, k], {"dp": at[k] * hop + lo})
                cp.start()
                spread.append(cp)

        pair_sum(0)
        if m > 1:
            pair_sum(1)
        send_all()
        for i in range(2, m):
            pair_sum(i)
        for k in range(1, far):
            spread[k].wait_recv()
            came = every.at[back[k] * hop + lo]
            cp = to(came, came, ags.at[0, k], ags.at[1, k], {"dp": near})
            cp.start()
            ending.append(cp)
        for cp in gz:
            cp.wait()
        acc = g_mine[1]
        for k in range(1, far):
            acc += g_land[k]
        for j, axis in enumerate(("col", "row")):
            g_mine[2 + j] = acc
            cp = to(
                g_mine.at[2 + j], g_land.at[far + j], gs.at[0, far + j], gs.at[1, far + j],
                {axis: 1 - lax.axis_index(axis)},
            )
            cp.start()
            cp.wait()
            acc = acc + g_land[far + j]
        gsum[...] = acc
        for i in range(1, m):
            outs[i - 1][...] = total(i)
        spread[0].wait()
        for cp in spread[1:]:
            cp.wait_send()
        for cp in ending:
            cp.wait()
        for cp in ycopy.values():
            cp.wait_send()
        for cp in zcopy.values():
            cp.wait_send()

    outs = [jax.ShapeDtypeStruct((n, t, w), BF16)]
    outs += [jax.ShapeDtypeStruct((t, w), F32)] * (m - 1)
    outs += [jax.ShapeDtypeStruct(gains.shape, F32)]
    dma = pltpu.SemaphoreType.DMA
    block = pltpu.VMEM((m, far, t, w), BF16)
    scratch = [
        block, block, block,
        pltpu.VMEM((4,) + gains.shape, F32),
        pltpu.VMEM((far + 2,) + gains.shape, F32),
        dma((2, m, far)), dma((2, m, far)), dma((4, far)), dma((2, far + 2)),
    ]
    return call(body, outs, scratch, list(arrays) + [gains], cid)


def head(values, h):
    return values[:, h * HEAD_SIZE : (h + 1) * HEAD_SIZE]


def turn(x, xp, cos, sin):
    x, xp = x.astype(F32), xp.astype(F32)
    return (x * cos + xp * sin).astype(BF16), (xp * cos - x * sin).astype(BF16)


def pick(flag, a, b):
    return jnp.where(flag, b, a)


def attn_forward(q, k, v, qp, kp, cos, sin, seg_col, seg_row, sel):
    heads = q.shape[1] // HEAD_SIZE
    t = q.shape[0]

    def body(sel, q, k, v, qp, kp, cos, sin, seg_c, seg_r, out, lt, qr, qrp, kr, krp):
        co, si = cos[...], sin[...]
        at = lax.broadcasted_iota(jnp.int32, (t, t), 0)
        to = lax.broadcasted_iota(jnp.int32, (t, t), 1)
        allowed = (seg_c[...] == seg_r[...]) & (to <= at)
        kk = []
        for g in range(2):
            a, b = turn(head(k, g), head(kp, g), co, si)
            kr[:, g * HEAD_SIZE : (g + 1) * HEAD_SIZE] = a
            krp[:, g * HEAD_SIZE : (g + 1) * HEAD_SIZE] = b
            kk.append(a)
        vv = [head(v, 0), head(v, 1)]
        for h in range(heads):
            a, b = turn(head(q, h), head(qp, h), co, si)
            qr[:, h * HEAD_SIZE : (h + 1) * HEAD_SIZE] = a
            qrp[:, h * HEAD_SIZE : (h + 1) * HEAD_SIZE] = b
            f = sel[h] == 1
            s = contract_cols(a, pick(f, *kk)) * HEAD_SIZE**-0.5
            s = jnp.where(allowed, s, masked_score)
            m = jnp.max(s, axis=1, keepdims=True)
            l = m + jnp.log(jnp.sum(jnp.exp(s - m), axis=1, keepdims=True))
            lt[:, h : h + 1] = l
            p = jnp.exp(s - l).astype(BF16)
            out[:, h * HEAD_SIZE : (h + 1) * HEAD_SIZE] = matmul(p, pick(f, *vv)).astype(BF16)

    outs = [
        jax.ShapeDtypeStruct(q.shape, BF16),
        jax.ShapeDtypeStruct((t, heads), F32),
        jax.ShapeDtypeStruct(q.shape, BF16),
        jax.ShapeDtypeStruct(q.shape, BF16),
        jax.ShapeDtypeStruct(k.shape, BF16),
        jax.ShapeDtypeStruct(k.shape, BF16),
    ]
    return pl.pallas_call(
        body,
        out_shape=outs,
        in_specs=[pl.BlockSpec(memory_space=pltpu.SMEM)] + [VM] * 9,
        out_specs=[VM] * 6,
        compiler_params=pltpu.CompilerParams(vmem_limit_bytes=60 * 2**20),
        name="attn_forward",
    )(sel, q, k, v, qp, kp, cos, sin, seg_col, seg_row)


def attn_back(sel, qr, qrp, kr, krp, v, lt, att, da, cos, sin, seg_c, seg_r, out):
    t, kw = kr.shape
    heads = qr.shape[1] // HEAD_SIZE
    co, si = cos[...], sin[...]
    at = lax.broadcasted_iota(jnp.int32, (t, t), 0)
    to = lax.broadcasted_iota(jnp.int32, (t, t), 1)
    allowed = (seg_c[...] == seg_r[...]) & (to <= at)
    kk = [jnp.concatenate([head(kr, g), head(krp, g)], axis=1) for g in range(2)]
    vv = [head(v, 0), head(v, 1)]
    dk = [jnp.zeros((t, 2 * HEAD_SIZE), F32)] * 2
    dv = [jnp.zeros((t, HEAD_SIZE), F32)] * 2
    for h in range(heads):
        f = sel[h] == 1
        kc = pick(f, *kk)
        vh = pick(f, *vv)
        qh = head(qr, h)
        dh = head(da, h)
        s = contract_cols(qh, kc[:, :HEAD_SIZE]) * HEAD_SIZE**-0.5
        s = jnp.where(allowed, s, masked_score)
        p = jnp.exp(s - lt[:, h : h + 1])
        dot = jnp.sum(dh.astype(F32) * head(att, h).astype(F32), axis=1, keepdims=True)
        dvh = contract_rows(p.astype(BF16), dh)
        dp = contract_cols(dh, vh)
        ds = (p * (dp - dot) * HEAD_SIZE**-0.5).astype(BF16)
        dq = matmul(ds, kc)
        dq = dq[:, :HEAD_SIZE] * co - dq[:, HEAD_SIZE:] * si
        out[:, h * HEAD_SIZE : (h + 1) * HEAD_SIZE] = dq.astype(BF16)
        dkh = contract_rows(ds, jnp.concatenate([qh, head(qrp, h)], axis=1))
        zk, zv = jnp.zeros_like(dkh), jnp.zeros_like(dvh)
        dk = [dk[0] + pick(f, dkh, zk), dk[1] + pick(f, zk, dkh)]
        dv = [dv[0] + pick(f, dvh, zv), dv[1] + pick(f, zv, dvh)]
    base = heads * HEAD_SIZE
    for g in range(2):
        lo = base + g * HEAD_SIZE
        back = dk[g][:, :HEAD_SIZE] * co - dk[g][:, HEAD_SIZE:] * si
        out[:, lo : lo + HEAD_SIZE] = back.astype(BF16)
        out[:, lo + kw : lo + kw + HEAD_SIZE] = dv[g].astype(BF16)


def tail(wgs, mids, attn, ins, outs_, cid):
    m = len(wgs)
    n, t, w = wgs[0].shape
    hop = 2
    far = n // hop
    args = list(wgs) + list(mids) + list(attn) + list(ins) + list(outs_)
    tokens = attn[0].shape[0]

    def body(*refs):
        g = refs[:m]
        part, mid, og, gain2, wo_mine = refs[m : m + 5]
        qr, qrp, kr, krp, v, lt, att, cos, sin, seg_c, seg_r = refs[m + 5 : m + 16]
        w_three, hid, gain1, part_out, my_mid = refs[m + 16 : m + 21]
        o = m + 21
        mg_all, gg2, pg, in_grad, gg1, h_out = refs[o : o + 6]
        totals = refs[o + 6 : o + 6 + m]
        sc = refs[o + 6 + m :]
        land, summed, got, ys, zs = sc[:5]
        s_mid, s_in, s_out = sc[5:9], sc[9:13], sc[13:17]
        da, part_in, mg, swap, swapped, ags, sws = sc[17:]
        me = lax.axis_index("dp")
        r, c = lax.axis_index("row"), lax.axis_index("col")
        hi, lo = me // hop, me % hop
        near = hi * hop + 1 - lo
        at = [lax.rem(hi + k, far) for k in range(far)]

        def to(src, dst, send, recv, dev):
            return pltpu.make_async_remote_copy(
                src_ref=src, dst_ref=dst, send_sem=send, recv_sem=recv,
                device_id=dev, device_id_type=MESH,
            )

        barrier = pltpu.get_barrier_semaphore()
        peers = [{"dp": near}] + [{"dp": at[k] * hop + lo} for k in range(1, far)]
        peers += [{"row": 1 - r}, {"col": 1 - c}]
        for dev in peers:
            pl.semaphore_signal(barrier, inc=1, device_id=dev, device_id_type=MESH)
        pl.semaphore_wait(barrier, len(peers))

        order = list(range(1, far)) + [0]
        ycopy, zcopy = {}, {}
        for i in range(m):
            for k in order:
                cp = to(
                    g[i].at[at[k] * hop + 1 - lo], land.at[i, k],
                    ys.at[0, i, k], ys.at[1, i, k], {"dp": near},
                )
                cp.start()
                ycopy[i, k] = cp

        def pair_sum(i):
            for k in order:
                ycopy[i, k].wait_recv()
                if k:
                    mine = g[i][at[k] * hop + lo].astype(F32)
                    summed[i, k] = (mine + land[i, k].astype(F32)).astype(BF16)
                    cp = to(
                        summed.at[i, k], got.at[i, k],
                        zs.at[0, i, k], zs.at[1, i, k], {"dp": at[k] * hop + lo},
                    )
                    cp.start()
                    zcopy[i, k] = cp

        total, end_mid = scatter_sum(part, *s_mid)
        back, gsum = norm_back(total, mid[...], gain2[...])
        back = back + og[...].astype(F32)
        mg_all[c, r] = back.astype(BF16)
        mine = mg_all.at[c, r]
        a = remote(mine, mine, ags.at[0], ags.at[1], "col")
        b = remote(mine, mine, ags.at[2], ags.at[3], "row")
        a.start()
        b.start()
        mg[...] = back
        gg2[...] = gsum
        pair_sum(0)
        a.wait_recv()
        theirs = mg_all.at[1 - c, r]
        f = remote(theirs, theirs, ags.at[4], ags.at[5], "row")
        f.start()
        a.wait_send()
        b.wait()
        f.wait()
        q4 = tokens // 4
        for i in range(4):
            da[i * q4 : (i + 1) * q4, :] = contract_cols(
                mg_all[i // 2, i % 2], wo_mine[...]
            ).astype(BF16)
        pair_sum(1)
        heads = qr.shape[1] // HEAD_SIZE
        group = QUERY_HEADS // KEY_VALUE_HEADS
        first = c * (QUERY_HEADS - 2 * heads) + r * heads
        sel = [(first + h) // group - first // group for h in range(heads)]
        attn_back(sel, qr, qrp, kr, krp, v, lt, att, da, cos, sin, seg_c, seg_r, pg)
        for i in range(4):
            part_in[i // 2, i % 2] = contract_cols(
                pg[i * q4 : (i + 1) * q4, :], w_three[...]
            ).astype(BF16)
        total, end_in = scatter_sum(part_in, *s_in)
        back, gsum = norm_back(total, hid[...].astype(F32), gain1[...])
        back = back + mg[...]
        hw = back.shape[1] // 2
        swap[0] = back[:, :hw]
        swap[1] = back[:, hw:]
        a = remote(swap.at[1 - r], swapped, sws.at[0], sws.at[1], "row")
        a.start()
        gg1[...] = gsum
        in_grad[r] = swap[r]
        for i in range(2, m):
            pair_sum(i)
        a.wait()
        in_grad[1 - r] = swapped[...]
        total, end_out = scatter_sum(part_out, *s_out)
        h_out[...] = (total + my_mid[...]).astype(BF16)
        for i in range(m):
            acc = g[i][me].astype(F32) + land[i, 0].astype(F32)
            for k in range(1, far):
                zcopy[i, k].wait_recv()
                acc += got[i, k].astype(F32)
            totals[i][...] = acc
        end_mid()
        end_in()
        end_out()
        for cp in ycopy.values():
            cp.wait_send()
        for cp in zcopy.values():
            cp.wait_send()

    part, mid = mids[0], mids[1]
    tq, width = mid.shape
    heads_w, kw = attn[0].shape[1], attn[2].shape[1]
    sd = jax.ShapeDtypeStruct
    outs = [
        sd((2, 2, tq, width), BF16),
        sd((1, width), F32),
        sd((tokens, heads_w + 2 * kw), BF16),
        sd((2, tq, width // 2), F32),
        sd((1, width), F32),
        sd(outs_[1].shape, BF16),
    ] + [sd((t, w), F32)] * m
    dma = pltpu.SemaphoreType.DMA
    block = pltpu.VMEM((m, far, t, w), BF16)
    scratch = [block, block, block, dma((2, m, far)), dma((2, m, far))]
    scratch += scatter_scratch(part) + scatter_scratch(part) + scatter_scratch(outs_[0])
    scratch += [
        pltpu.VMEM((tokens, heads_w), BF16),
        pltpu.VMEM(part.shape, BF16),
        pltpu.VMEM((tq, width), F32),
        pltpu.VMEM((2, tq, width // 2), F32),
        pltpu.VMEM((tq, width // 2), F32),
        dma((6,)),
        dma((2,)),
    ]
    return call(body, outs, scratch, args, cid)


def swap_halves(weights):
    w = weights.reshape(weights.shape[0], -1, 2, HEAD_SIZE // 2)
    return jnp.concatenate([-w[:, :, 1:], w[:, :, :1]], axis=2).reshape(weights.shape)


def flat(slots):
    a, b, t, w = slots.shape
    return jnp.transpose(slots, (0, 2, 1, 3)).reshape(a * t, b * w)


def ordered(r, mine, theirs, axis):
    return jnp.where(
        r == 0,
        jnp.concatenate([mine, theirs], axis=axis),
        jnp.concatenate([theirs, mine], axis=axis),
    )


PAIR = [(0, 1), (1, 0)]


def on_device(
    hidden_in,
    segment_ids,
    position_ids,
    attn_gain,
    query_weight,
    key_weight,
    value_matrix,
    output_weight,
    ffn_gain,
    gate_weight,
    up_weight,
    down_weight,
    out_grad,
):
    r, c = lax.axis_index("row"), lax.axis_index("col")
    t = segment_ids.shape[0]
    width = 2 * hidden_in.shape[1]
    qc, kc = query_weight.shape[1], key_weight.shape[1]
    half = qc % HEAD_SIZE
    fw = gate_weight.shape[1] // 2
    slots_q = (qc + half) // 2
    slots_k = 2 * HEAD_SIZE

    def edge_of(w):
        n = w.shape[1]
        return jnp.where(c == 0, w[:, n - half :], w[:, :half])

    own = jnp.concatenate([query_weight, key_weight, value_matrix], axis=1)
    edge = jnp.concatenate(
        [edge_of(query_weight), edge_of(key_weight), edge_of(value_matrix)], axis=1
    )
    gains = jnp.stack([attn_gain, ffn_gain])
    h_s, edge_s, gain_s, own_s, gate_s, up_s, down_s = exchange(
        ("all", "all", "row", "row", "cols", "cols", "lead"),
        [
            hidden_in,
            edge,
            gains,
            own,
            gate_weight,
            up_weight,
            down_weight.reshape(2, fw, down_weight.shape[1]),
        ],
        1,
    )
    output_weight, out_grad, h_s = lax.optimization_barrier((output_weight, out_grad, h_s))
    wo_x = lax.ppermute(output_weight, "col", PAIR)
    og_x = lax.ppermute(out_grad, "col", PAIR)
    gains = jnp.transpose(gain_s, (1, 0, 2)).reshape(2, width)
    g_one, g_two = gains[0:1], gains[1:2]
    hid = flat(h_s)
    resid = hid.astype(F32)

    frequency = rope_base ** (
        -(jnp.arange(HEAD_SIZE // 2, dtype=F32) * 2.0) / HEAD_SIZE
    )
    angles = position_ids.astype(F32)[:, None] * frequency[None, :]
    cos, sin = jnp.cos(angles), jnp.sin(angles)
    cos = jnp.concatenate([cos, cos], axis=1)
    sin = jnp.concatenate([sin, sin], axis=1)

    own = own_s.reshape(width, qc + 2 * kc)
    edge_x = lax.dynamic_index_in_dim(edge_s, 1 - c, 0, keepdims=False).reshape(width, 3 * half)

    def local(lo, n, e, size):
        ext = ordered(c, own[:, lo : lo + n], edge_x[:, e * half : (e + 1) * half], 1)
        step = (ext.shape[1] - size)
        return lax.dynamic_slice_in_dim(ext, r * step, size, 1)

    wq = local(0, qc, 0, slots_q)
    wk = local(qc, kc, 1, slots_k)
    wv = local(qc + kc, kc, 2, slots_k)
    w_three = jnp.concatenate([wq, wk, wv], axis=1)
    w_all = jnp.concatenate([w_three, swap_halves(wq), swap_halves(wk)], axis=1)
    inv_one = lax.rsqrt(jnp.mean(resid * resid, axis=1, keepdims=True) + epsilon)
    normed_one = (resid * inv_one * g_one).astype(BF16)
    proj = matmul(normed_one, w_all).astype(BF16)
    e1, e2, e3, e4 = slots_q, slots_q + slots_k, slots_q + 2 * slots_k, 2 * slots_q + 2 * slots_k
    q, k, v, qp, kp = proj[:, :e1], proj[:, e1:e2], proj[:, e2:e3], proj[:, e3:e4], proj[:, e4:]
    heads = slots_q // HEAD_SIZE
    group = QUERY_HEADS // KEY_VALUE_HEADS
    first = c * (QUERY_HEADS - 2 * heads) + r * heads
    sel = (first + jnp.arange(heads, dtype=jnp.int32)) // group - first // group
    seg_col, seg_row = segment_ids[:, None], segment_ids[None, :]
    att, lt, qr, qrp, kr, krp = attn_forward(q, k, v, qp, kp, cos, sin, seg_col, seg_row, sel)

    pair_wo = jnp.stack([output_weight, wo_x])
    pair_og = jnp.stack([out_grad, og_x])
    att_s, wo_s, og_s = exchange(("all", "row", "row"), [att, pair_wo, pair_og], 2)
    def cols_first(s):
        s = jnp.where(c == 0, s, s[:, ::-1])
        return jnp.transpose(s, (1, 0, 2, 3))

    wo = flat(cols_first(wo_s))
    og = flat(cols_first(og_s))
    att_all = jnp.transpose(att_s.reshape(4, t, slots_q), (1, 0, 2)).reshape(t, 4 * slots_q)
    wo_pad = jnp.concatenate(
        [wo[: 2 * slots_q], jnp.zeros((HEAD_SIZE, width), BF16), wo[2 * slots_q :]], axis=0
    )
    mid = resid + matmul(att_all, wo_pad)
    inv_two = lax.rsqrt(jnp.mean(mid * mid, axis=1, keepdims=True) + epsilon)
    normed_two = (mid * inv_two * g_two).astype(BF16)
    gate_w = gate_s.reshape(width, fw)
    up_w = up_s.reshape(width, fw)
    gate = matmul(normed_two, gate_w)
    up = matmul(normed_two, up_w)
    sig = jax.nn.sigmoid(gate)
    silu = gate * sig
    inner = (silu * up).astype(BF16)
    down_w = jnp.transpose(down_s, (1, 0, 2)).reshape(fw, width)
    inner_grad = contract_cols(og, down_w)
    gate_grad = (inner_grad * up * sig * (1.0 + gate * (1.0 - sig))).astype(BF16)
    up_grad = (inner_grad * silu).astype(BF16)
    both = jnp.concatenate([gate_grad, up_grad], axis=1)
    both_w = jnp.concatenate([gate_w, up_w], axis=1)
    part_two = contract_cols(both, both_w).astype(BF16).reshape(2, 2, t // 4, width)

    slot = 2 * c + r
    def quarter(x):
        return lax.dynamic_slice_in_dim(x, slot * (t // 4), t // 4, 0)

    def row_half(x):
        return lax.dynamic_slice_in_dim(x, r * (width // 2), width // 2, 1)

    hand = jnp.concatenate([both, inner], axis=1)
    hand_x = lax.ppermute(hand, "row", PAIR)
    gate_full = ordered(r, hand[:, :fw], hand_x[:, :fw], 1)
    up_full = ordered(r, hand[:, fw : 2 * fw], hand_x[:, fw : 2 * fw], 1)
    inner_full = ordered(r, hand[:, 2 * fw :], hand_x[:, 2 * fw :], 1)
    n2 = row_half(normed_two)
    n_dp = lax.axis_size("dp")
    gate_wg = contract_rows(gate_full, n2).astype(BF16)
    up_wg = contract_rows(up_full, n2).astype(BF16)
    down_wg = contract_rows(inner_full, row_half(og)).astype(BF16)

    def blocks(x):
        return x.reshape(n_dp, x.shape[0] // n_dp, x.shape[1])

    part_out = jnp.stack(
        [matmul(inner, down_s[0]).astype(BF16), matmul(inner, down_s[1]).astype(BF16)]
    ).reshape(2, 2, t // 2, width // 2)
    part_out = jnp.transpose(part_out, (1, 0, 2, 3))
    my_mid = lax.dynamic_slice(mid, (c * (t // 2), r * (width // 2)), (t // 2, width // 2))
    wo_mine = lax.dynamic_slice_in_dim(wo_pad, slot * slots_q, slots_q, 0)
    mg_s, gg_two, pg, in_grad, gg_one, hidden_out, down_t, gate_t, up_t = tail(
        [blocks(down_wg), blocks(gate_wg), blocks(up_wg)],
        [part_two, quarter(mid), quarter(og), g_two, wo_mine],
        [qr, qrp, kr, krp, v, lt, att, cos, sin, seg_col, seg_row],
        [w_three, quarter(hid), g_one],
        [part_out, my_mid],
        3,
    )
    mg_all = mg_s.reshape(t, width)
    hidden_in_grad = in_grad.reshape(t // 2, width // 2)

    att15 = jnp.concatenate(
        [att_all[:, : 2 * slots_q], att_all[:, 2 * slots_q + HEAD_SIZE :]], axis=1
    )
    att_c = lax.dynamic_slice_in_dim(att15, c * qc, qc, 1)
    out_wg = contract_rows(att_c, row_half(mg_all))
    pg_x = lax.ppermute(pg, "row", PAIR)
    pg0 = jnp.where(r == 0, pg, pg_x).astype(F32)
    pg1 = jnp.where(r == 0, pg_x, pg).astype(F32)
    ext_q = jnp.concatenate([pg0[:, :e1], pg1[:, :e1]], axis=1)

    def ext_of(lo):
        z = jnp.zeros((t, HEAD_SIZE), F32)
        a, b = pg0[:, lo : lo + slots_k], pg1[:, lo : lo + slots_k]
        return jnp.concatenate([a, z], axis=1) + jnp.concatenate([z, b], axis=1)

    exts = [ext_q, ext_of(e1), ext_of(e2)]
    sends = [jnp.where(c == 0, x[:, -half:], x[:, :half]) for x in exts]
    got = lax.ppermute(jnp.concatenate(sends, axis=1).astype(BF16), "col", PAIR).astype(F32)
    finals = []
    for i, x in enumerate(exts):
        n = x.shape[1]
        g = got[:, i * half : (i + 1) * half]
        low = jnp.concatenate([x[:, : n - 2 * half], x[:, n - 2 * half : n - half] + g], axis=1)
        high = jnp.concatenate([x[:, half : 2 * half] + g, x[:, 2 * half :]], axis=1)
        finals.append(jnp.where(c == 0, low, high).astype(BF16))
    proj_wg = contract_rows(jnp.concatenate(finals, axis=1), row_half(normed_one))
    attn_wg = jnp.concatenate([proj_wg.astype(BF16), out_wg.astype(BF16)], axis=0)
    gain_part = jnp.concatenate([gg_one, gg_two], axis=0)
    attn_t, gain_t = dp_reduce([blocks(attn_wg)], gain_part, 6)
    gain_t = row_half(gain_t)
    attn_t = attn_t.reshape(attn_wg.shape)
    n_proj = qc + 2 * kc
    proj_t = attn_t[:n_proj].T.astype(F32)
    out_t = attn_t[n_proj:]
    gate_t, up_t, down_t = gate_t.T[None], up_t.T[None], down_t[None]
    return (
        hidden_out,
        hidden_in_grad,
        gain_t[0],
        proj_t[:, :qc],
        proj_t[:, qc : qc + kc],
        proj_t[:, qc + kc :],
        out_t.astype(F32),
        gain_t[1],
        gate_t,
        up_t,
        down_t,
    )


def solution(mesh):
    return jax.shard_map(
        on_device,
        mesh=mesh,
        in_specs=(
            P(("dp", "col"), "row"),
            P("dp"),
            P("dp"),
            P("row"),
            P("row", "col"),
            P("row", "col"),
            P("row", "col"),
            P("col", "row"),
            P("row"),
            P("row", "col"),
            P("row", "col"),
            P("col", "row"),
            P(("dp", "col"), "row"),
        ),
        out_specs=(
            P(("dp", "col"), "row"),
            P(("dp", "col"), "row"),
            P("row"),
            P("row", "col"),
            P("row", "col"),
            P("row", "col"),
            P("col", "row"),
            P("row"),
            P("col", "row", "dp"),
            P("col", "row", "dp"),
            P("col", "dp", "row"),
        ),
        check_vma=False,
    )
```

```python
import functools

import jax
import jax.numpy as jnp
from jax import lax
from jax.experimental import pallas as pl
from jax.experimental.pallas import tpu as pltpu
from jax.sharding import PartitionSpec as P

HEAD_SIZE = 64
QUERY_HEADS = 15
KEY_VALUE_HEADS = 5
epsilon = 1e-05
rope_base = 10000.0
masked_score = -1e30
MESH = pl.DeviceIdType.MESH
F32 = jnp.float32
BF16 = jnp.bfloat16
VM = pl.BlockSpec(memory_space=pltpu.VMEM)


def matmul(left, right):
    return jnp.dot(left, right, preferred_element_type=F32)


def contract_rows(left, right):
    return lax.dot_general(left, right, (((0,), (0,)), ((), ())), preferred_element_type=F32)


def contract_cols(left, right):
    return lax.dot_general(left, right, (((1,), (1,)), ((), ())), preferred_element_type=F32)


def greet(axes):
    barrier = pltpu.get_barrier_semaphore()
    for axis in axes:
        other = 1 - lax.axis_index(axis)
        pl.semaphore_signal(barrier, inc=1, device_id={axis: other}, device_id_type=MESH)
    pl.semaphore_wait(barrier, len(axes))


def remote(src, dst, send_sem, recv_sem, axis):
    return pltpu.make_async_remote_copy(
        src_ref=src,
        dst_ref=dst,
        send_sem=send_sem,
        recv_sem=recv_sem,
        device_id={axis: 1 - lax.axis_index(axis)},
        device_id_type=MESH,
    )


def call(body, outs, scratch, args, cid, vmem=60 * 2**20):
    return pl.pallas_call(
        body,
        out_shape=outs,
        in_specs=[VM] * len(args),
        out_specs=[VM] * len(outs),
        scratch_shapes=scratch,
        compiler_params=pltpu.CompilerParams(
            collective_id=cid, has_side_effects=cid is not None, vmem_limit_bytes=vmem
        ),
    )(*args)


def exchange(kinds, arrays, cid, forms=None):
    n = len(arrays)
    forms = forms or ("",) * n
    lands = [i for i in range(n) if forms[i]]
    shown = [i for i in range(n) if forms[i] != "-"]

    def body(*refs):
        ins, finals, sems = refs[:n], refs[n : n + len(shown)], refs[n + len(shown)]
        outs = [None] * n
        for i, ref in zip(shown, finals):
            outs[i] = ref
        for i, ref in zip(lands, refs[n + len(shown) + 1 :]):
            outs[i] = ref
        r, c = lax.axis_index("row"), lax.axis_index("col")
        greet(("row", "col") if "all" in kinds else ("row",))
        pending, firsts = [], []
        for i, kind in enumerate(kinds):
            if kind == "all":
                cp = remote(ins[i], outs[i].at[c, r], sems.at[i, 0], sems.at[i, 1], "col")
                cp.start()
                firsts.append((i, cp))
        for i, kind in enumerate(kinds):
            if kind == "all":
                src, keep, dst = ins[i], ins[i], outs[i].at[c, r]
            elif kind == "row":
                src, keep, dst = ins[i], ins[i], outs[i].at[r]
            elif kind == "lead":
                src, keep, dst = ins[i].at[1 - r], ins[i].at[r], outs[i].at[r]
            else:
                w = ins[i].shape[1] // 2
                src = ins[i].at[:, pl.ds(pl.multiple_of((1 - r) * w, 128), w)]
                keep = ins[i].at[:, pl.ds(pl.multiple_of(r * w, 128), w)]
                dst = outs[i].at[r]
            cp = remote(src, dst, sems.at[i, 2], sems.at[i, 3], "row")
            cp.start()
            loc = pltpu.make_async_copy(keep, dst, sems.at[i, 6])
            loc.start()
            pending += [cp, loc]
        for i, cp in firsts:
            cp.wait_recv()
            fw = remote(
                outs[i].at[1 - c, r], outs[i].at[1 - c, r], sems.at[i, 4], sems.at[i, 5], "row"
            )
            fw.start()
            pending.append(fw)
        for _, cp in firsts:
            cp.wait_send()
        for cp in pending:
            cp.wait()
        for i, out in zip(shown, finals):
            form, land = forms[i], outs[i]
            if not form:
                continue
            h, w = land.shape[-2:]
            for a in range(2):
                for b in range(2):
                    if form == "square":
                        out[a * h : (a + 1) * h, b * w : (b + 1) * w] = land[a, b]
                    elif form == "line":
                        j = 2 * a + b
                        out[:, j * w : (j + 1) * w] = land[a, b]
                    elif form == "pair":
                        value = jnp.where(c == a, land[b], outs[i + 1][b])
                        out[a * h : (a + 1) * h, b * w : (b + 1) * w] = value
                if form == "wide":
                    out[:, a * w : (a + 1) * w] = land[a]

    outs = []
    for kind, a in zip(kinds, arrays):
        if kind == "all":
            s = (2, 2) + a.shape
        elif kind == "row":
            s = (2,) + a.shape
        elif kind == "lead":
            s = a.shape
        else:
            s = (2, a.shape[0], a.shape[1] // 2)
        outs.append(jax.ShapeDtypeStruct(s, a.dtype))
    scale = {"square": (2, 2), "line": (1, 4), "pair": (2, 2), "wide": (1, 2)}
    scratch = [pltpu.SemaphoreType.DMA((n, 7))]
    scratch += [pltpu.VMEM(outs[i].shape, outs[i].dtype) for i in lands]
    for i in lands:
        if forms[i] != "-":
            x, y = scale[forms[i]]
            h, w = outs[i].shape[-2:]
            outs[i] = jax.ShapeDtypeStruct((h * x, w * y), outs[i].dtype)
    return call(body, [outs[i] for i in shown], scratch, arrays, cid)


def scatter_scratch(part):
    s, d = part.shape[2:], part.dtype
    return [
        pltpu.VMEM((2,) + s, d),
        pltpu.VMEM(s, d),
        pltpu.VMEM(s, d),
        pltpu.SemaphoreType.DMA((6,)),
    ]


def scatter_sum(part, land, out_x, land_x, sems):
    r, c = lax.axis_index("row"), lax.axis_index("col")
    first = remote(part.at[1 - c, 1 - r], land.at[0], sems.at[0], sems.at[1], "row")
    second = remote(part.at[c, 1 - r], land.at[1], sems.at[2], sems.at[3], "row")
    first.start()
    second.start()
    first.wait_recv()
    out_x[...] = (part[1 - c, r].astype(F32) + land[0].astype(F32)).astype(out_x.dtype)
    third = remote(out_x, land_x, sems.at[4], sems.at[5], "col")
    third.start()
    second.wait_recv()
    mine = part[c, r].astype(F32) + land[1].astype(F32)
    third.wait_recv()
    total = mine + land_x[...].astype(F32)

    def finish():
        first.wait_send()
        second.wait_send()
        third.wait_send()

    return total, finish


def norm_back(grad, resid, gain):
    width = resid.shape[1]
    inv = lax.rsqrt(jnp.sum(resid * resid, axis=1, keepdims=True) / width + epsilon)
    unit = resid * inv
    weighted = grad * gain
    mean = jnp.sum(weighted * unit, axis=1, keepdims=True) / width
    return inv * (weighted - unit * mean), jnp.sum(grad * unit, axis=0, keepdims=True)


def dp_reduce(arrays, gains, cid):
    m = len(arrays)
    n, t, w = arrays[0].shape
    hop = 2
    far = n // hop

    def body(*refs):
        g, gain = refs[:m], refs[m]
        every, outs, gsum = refs[m + 1], refs[m + 2 : 2 * m + 1], refs[2 * m + 1]
        land, summed, got, g_mine, g_land, ys, zs, ags, gs = refs[2 * m + 2 :]
        me = lax.axis_index("dp")
        hi, lo = me // hop, me % hop
        near = hi * hop + 1 - lo
        at = [lax.rem(hi + k, far) for k in range(far)]
        back = [lax.rem(hi + far - k, far) for k in range(far)]

        def to(src, dst, send, recv, dev):
            return pltpu.make_async_remote_copy(
                src_ref=src, dst_ref=dst, send_sem=send, recv_sem=recv,
                device_id=dev, device_id_type=MESH,
            )

        barrier = pltpu.get_barrier_semaphore()
        peers = [{"dp": near}] + [{"dp": at[k] * hop + lo} for k in range(1, far)]
        peers += [{a: 1 - lax.axis_index(a)} for a in ("row", "col")]
        for dev in peers:
            pl.semaphore_signal(barrier, inc=1, device_id=dev, device_id_type=MESH)
        pl.semaphore_wait(barrier, len(peers))

        ending = []
        g_mine[0] = gain[...]
        gy = to(g_mine.at[0], g_land.at[0], gs.at[0, 0], gs.at[1, 0], {"dp": near})
        gy.start()
        order = list(range(1, far)) + [0]
        ycopy, zcopy = {}, {}
        for i in range(m):
            for k in order:
                cp = to(
                    g[i].at[at[k] * hop + 1 - lo], land.at[i, k],
                    ys.at[0, i, k], ys.at[1, i, k], {"dp": near},
                )
                cp.start()
                ycopy[i, k] = cp
        gy.wait()
        g_mine[1] = g_mine[0] + g_land[0]
        gz = []
        for k in range(1, far):
            cp = to(
                g_mine.at[1], g_land.at[k], gs.at[0, k], gs.at[1, k], {"dp": at[k] * hop + lo}
            )
            cp.start()
            gz.append(cp)

        def pair_sum(i):
            for k in order:
                ycopy[i, k].wait_recv()
                if k:
                    mine = g[i][at[k] * hop + lo].astype(F32)
                    summed[i, k] = (mine + land[i, k].astype(F32)).astype(BF16)
                    cp = to(
                        summed.at[i, k], got.at[i, k],
                        zs.at[0, i, k], zs.at[1, i, k], {"dp": at[k] * hop + lo},
                    )
                    cp.start()
                    zcopy[i, k] = cp

        def total(i):
            acc = g[i][me].astype(F32) + land[i, 0].astype(F32)
            for k in range(1, far):
                zcopy[i, k].wait_recv()
                acc += got[i, k].astype(F32)
            return acc

        spread = []

        def send_all():
            every[me] = total(0).astype(BF16)
            mine = every.at[me]
            cp = to(mine, mine, ags.at[0, 0], ags.at[1, 0], {"dp": near})
            cp.start()
            spread.append(cp)
            for k in range(1, far):
                cp = to(mine, mine, ags.at[2, k], ags.at[3, k], {"dp": at[k] * hop + lo})
                cp.start()
                spread.append(cp)

        pair_sum(0)
        if m > 1:
            pair_sum(1)
        send_all()
        for i in range(2, m):
            pair_sum(i)
        for k in range(1, far):
            spread[k].wait_recv()
            came = every.at[back[k] * hop + lo]
            cp = to(came, came, ags.at[0, k], ags.at[1, k], {"dp": near})
            cp.start()
            ending.append(cp)
        for cp in gz:
            cp.wait()
        acc = g_mine[1]
        for k in range(1, far):
            acc += g_land[k]
        for j, axis in enumerate(("col", "row")):
            g_mine[2 + j] = acc
            cp = to(
                g_mine.at[2 + j], g_land.at[far + j], gs.at[0, far + j], gs.at[1, far + j],
                {axis: 1 - lax.axis_index(axis)},
            )
            cp.start()
            cp.wait()
            acc = acc + g_land[far + j]
        gsum[...] = acc
        for i in range(1, m):
            outs[i - 1][...] = total(i)
        spread[0].wait()
        for cp in spread[1:]:
            cp.wait_send()
        for cp in ending:
            cp.wait()
        for cp in ycopy.values():
            cp.wait_send()
        for cp in zcopy.values():
            cp.wait_send()

    outs = [jax.ShapeDtypeStruct((n, t, w), BF16)]
    outs += [jax.ShapeDtypeStruct((t, w), F32)] * (m - 1)
    outs += [jax.ShapeDtypeStruct(gains.shape, F32)]
    dma = pltpu.SemaphoreType.DMA
    block = pltpu.VMEM((m, far, t, w), BF16)
    scratch = [
        block, block, block,
        pltpu.VMEM((4,) + gains.shape, F32),
        pltpu.VMEM((far + 2,) + gains.shape, F32),
        dma((2, m, far)), dma((2, m, far)), dma((4, far)), dma((2, far + 2)),
    ]
    return call(body, outs, scratch, list(arrays) + [gains], cid)


def head(values, h):
    return values[:, h * HEAD_SIZE : (h + 1) * HEAD_SIZE]


def turn(x, xp, cos, sin):
    x, xp = x.astype(F32), xp.astype(F32)
    return (x * cos + xp * sin).astype(BF16), (xp * cos - x * sin).astype(BF16)


def pick(flag, a, b):
    return jnp.where(flag, b, a)


def attn_forward(q, k, v, qp, kp, cos, sin, seg_col, seg_row, sel):
    heads = q.shape[1] // HEAD_SIZE
    t = q.shape[0]

    def body(sel, q, k, v, qp, kp, cos, sin, seg_c, seg_r, out, lt, qr, qrp, kr, krp):
        co, si = cos[...], sin[...]
        at = lax.broadcasted_iota(jnp.int32, (t, t), 0)
        to = lax.broadcasted_iota(jnp.int32, (t, t), 1)
        allowed = (seg_c[...] == seg_r[...]) & (to <= at)
        kk = []
        for g in range(2):
            a, b = turn(head(k, g), head(kp, g), co, si)
            kr[:, g * HEAD_SIZE : (g + 1) * HEAD_SIZE] = a
            krp[:, g * HEAD_SIZE : (g + 1) * HEAD_SIZE] = b
            kk.append(a)
        vv = [head(v, 0), head(v, 1)]
        for h in range(heads):
            a, b = turn(head(q, h), head(qp, h), co, si)
            qr[:, h * HEAD_SIZE : (h + 1) * HEAD_SIZE] = a
            qrp[:, h * HEAD_SIZE : (h + 1) * HEAD_SIZE] = b
            f = sel[h] == 1
            s = contract_cols(a, pick(f, *kk)) * HEAD_SIZE**-0.5
            s = jnp.where(allowed, s, masked_score)
            m = jnp.max(s, axis=1, keepdims=True)
            l = m + jnp.log(jnp.sum(jnp.exp(s - m), axis=1, keepdims=True))
            lt[:, h : h + 1] = l
            p = jnp.exp(s - l).astype(BF16)
            out[:, h * HEAD_SIZE : (h + 1) * HEAD_SIZE] = matmul(p, pick(f, *vv)).astype(BF16)

    outs = [
        jax.ShapeDtypeStruct(q.shape, BF16),
        jax.ShapeDtypeStruct((t, heads), F32),
        jax.ShapeDtypeStruct(q.shape, BF16),
        jax.ShapeDtypeStruct(q.shape, BF16),
        jax.ShapeDtypeStruct(k.shape, BF16),
        jax.ShapeDtypeStruct(k.shape, BF16),
    ]
    return pl.pallas_call(
        body,
        out_shape=outs,
        in_specs=[pl.BlockSpec(memory_space=pltpu.SMEM)] + [VM] * 9,
        out_specs=[VM] * 6,
        compiler_params=pltpu.CompilerParams(vmem_limit_bytes=60 * 2**20),
        name="attn_forward",
    )(sel, q, k, v, qp, kp, cos, sin, seg_col, seg_row)


def attn_back(sel, qr, qrp, kr, krp, v, lt, att, da, cos, sin, seg_c, seg_r, out):
    t, kw = kr.shape
    heads = qr.shape[1] // HEAD_SIZE
    co, si = cos[...], sin[...]
    at = lax.broadcasted_iota(jnp.int32, (t, t), 0)
    to = lax.broadcasted_iota(jnp.int32, (t, t), 1)
    allowed = (seg_c[...] == seg_r[...]) & (to <= at)
    kk = [jnp.concatenate([head(kr, g), head(krp, g)], axis=1) for g in range(2)]
    vv = [head(v, 0), head(v, 1)]
    dk = [jnp.zeros((t, 2 * HEAD_SIZE), F32)] * 2
    dv = [jnp.zeros((t, HEAD_SIZE), F32)] * 2
    for h in range(heads):
        f = sel[h] == 1
        kc = pick(f, *kk)
        vh = pick(f, *vv)
        qh = head(qr, h)
        dh = head(da, h)
        s = contract_cols(qh, kc[:, :HEAD_SIZE]) * HEAD_SIZE**-0.5
        s = jnp.where(allowed, s, masked_score)
        p = jnp.exp(s - lt[:, h : h + 1])
        dot = jnp.sum(dh.astype(F32) * head(att, h).astype(F32), axis=1, keepdims=True)
        dvh = contract_rows(p.astype(BF16), dh)
        dp = contract_cols(dh, vh)
        ds = (p * (dp - dot) * HEAD_SIZE**-0.5).astype(BF16)
        dq = matmul(ds, kc)
        dq = dq[:, :HEAD_SIZE] * co - dq[:, HEAD_SIZE:] * si
        out[:, h * HEAD_SIZE : (h + 1) * HEAD_SIZE] = dq.astype(BF16)
        dkh = contract_rows(ds, jnp.concatenate([qh, head(qrp, h)], axis=1))
        zk, zv = jnp.zeros_like(dkh), jnp.zeros_like(dvh)
        dk = [dk[0] + pick(f, dkh, zk), dk[1] + pick(f, zk, dkh)]
        dv = [dv[0] + pick(f, dvh, zv), dv[1] + pick(f, zv, dvh)]
    base = heads * HEAD_SIZE
    for g in range(2):
        lo = base + g * HEAD_SIZE
        back = dk[g][:, :HEAD_SIZE] * co - dk[g][:, HEAD_SIZE:] * si
        out[:, lo : lo + HEAD_SIZE] = back.astype(BF16)
        out[:, lo + kw : lo + kw + HEAD_SIZE] = dv[g].astype(BF16)


def tail(wgs, mids, attn, ins, outs_, cid):
    m = len(wgs)
    n, t, w = wgs[0].shape
    hop = 2
    far = n // hop
    args = list(wgs) + list(mids) + list(attn) + list(ins) + list(outs_)
    tokens = attn[0].shape[0]

    def body(*refs):
        g = refs[:m]
        part, mid, og, gain2, wo_mine = refs[m : m + 5]
        qr, qrp, kr, krp, v, lt, att, cos, sin, seg_c, seg_r = refs[m + 5 : m + 16]
        w_three, hid, gain1, part_out, my_mid = refs[m + 16 : m + 21]
        o = m + 21
        mg_all, gg2, pg, in_grad, gg1, h_out = refs[o : o + 6]
        totals = refs[o + 6 : o + 6 + m]
        sc = refs[o + 6 + m :]
        land, summed, got, ys, zs = sc[:5]
        s_mid, s_in, s_out = sc[5:9], sc[9:13], sc[13:17]
        da, part_in, mg, swap, swapped, ags, sws = sc[17:]
        me = lax.axis_index("dp")
        r, c = lax.axis_index("row"), lax.axis_index("col")
        hi, lo = me // hop, me % hop
        near = hi * hop + 1 - lo
        at = [lax.rem(hi + k, far) for k in range(far)]

        def to(src, dst, send, recv, dev):
            return pltpu.make_async_remote_copy(
                src_ref=src, dst_ref=dst, send_sem=send, recv_sem=recv,
                device_id=dev, device_id_type=MESH,
            )

        barrier = pltpu.get_barrier_semaphore()
        peers = [{"dp": near}] + [{"dp": at[k] * hop + lo} for k in range(1, far)]
        peers += [{"row": 1 - r}, {"col": 1 - c}]
        for dev in peers:
            pl.semaphore_signal(barrier, inc=1, device_id=dev, device_id_type=MESH)
        pl.semaphore_wait(barrier, len(peers))

        order = list(range(1, far)) + [0]
        ycopy, zcopy = {}, {}
        for i in range(m):
            for k in order:
                cp = to(
                    g[i].at[at[k] * hop + 1 - lo], land.at[i, k],
                    ys.at[0, i, k], ys.at[1, i, k], {"dp": near},
                )
                cp.start()
                ycopy[i, k] = cp

        def pair_sum(i):
            for k in order:
                ycopy[i, k].wait_recv()
                if k:
                    mine = g[i][at[k] * hop + lo].astype(F32)
                    summed[i, k] = (mine + land[i, k].astype(F32)).astype(BF16)
                    cp = to(
                        summed.at[i, k], got.at[i, k],
                        zs.at[0, i, k], zs.at[1, i, k], {"dp": at[k] * hop + lo},
                    )
                    cp.start()
                    zcopy[i, k] = cp

        total, end_mid = scatter_sum(part, *s_mid)
        back, gsum = norm_back(total, mid[...], gain2[...])
        back = back + og[...].astype(F32)
        mg_all[c, r] = back.astype(BF16)
        mine = mg_all.at[c, r]
        a = remote(mine, mine, ags.at[0], ags.at[1], "col")
        b = remote(mine, mine, ags.at[2], ags.at[3], "row")
        a.start()
        b.start()
        mg[...] = back
        gg2[...] = gsum
        pair_sum(0)
        a.wait_recv()
        theirs = mg_all.at[1 - c, r]
        f = remote(theirs, theirs, ags.at[4], ags.at[5], "row")
        f.start()
        a.wait_send()
        b.wait()
        f.wait()
        q4 = tokens // 4
        for i in range(4):
            da[i * q4 : (i + 1) * q4, :] = contract_cols(
                mg_all[i // 2, i % 2], wo_mine[...]
            ).astype(BF16)
        pair_sum(1)
        heads = qr.shape[1] // HEAD_SIZE
        group = QUERY_HEADS // KEY_VALUE_HEADS
        first = c * (QUERY_HEADS - 2 * heads) + r * heads
        sel = [(first + h) // group - first // group for h in range(heads)]
        attn_back(sel, qr, qrp, kr, krp, v, lt, att, da, cos, sin, seg_c, seg_r, pg)
        for i in range(4):
            part_in[i // 2, i % 2] = contract_cols(
                pg[i * q4 : (i + 1) * q4, :], w_three[...]
            ).astype(BF16)
        total, end_in = scatter_sum(part_in, *s_in)
        back, gsum = norm_back(total, hid[...].astype(F32), gain1[...])
        back = back + mg[...]
        hw = back.shape[1] // 2
        swap[0] = back[:, :hw]
        swap[1] = back[:, hw:]
        a = remote(swap.at[1 - r], swapped, sws.at[0], sws.at[1], "row")
        a.start()
        gg1[...] = gsum
        in_grad[r] = swap[r]
        for i in range(2, m):
            pair_sum(i)
        a.wait()
        in_grad[1 - r] = swapped[...]
        total, end_out = scatter_sum(part_out, *s_out)
        h_out[...] = (total + my_mid[...]).astype(BF16)
        for i in range(m):
            acc = g[i][me].astype(F32) + land[i, 0].astype(F32)
            for k in range(1, far):
                zcopy[i, k].wait_recv()
                acc += got[i, k].astype(F32)
            totals[i][...] = acc
        end_mid()
        end_in()
        end_out()
        for cp in ycopy.values():
            cp.wait_send()
        for cp in zcopy.values():
            cp.wait_send()

    part, mid = mids[0], mids[1]
    tq, width = mid.shape
    heads_w, kw = attn[0].shape[1], attn[2].shape[1]
    sd = jax.ShapeDtypeStruct
    outs = [
        sd((2, 2, tq, width), BF16),
        sd((1, width), F32),
        sd((tokens, heads_w + 2 * kw), BF16),
        sd((2, tq, width // 2), F32),
        sd((1, width), F32),
        sd(outs_[1].shape, BF16),
    ] + [sd((t, w), F32)] * m
    dma = pltpu.SemaphoreType.DMA
    block = pltpu.VMEM((m, far, t, w), BF16)
    scratch = [block, block, block, dma((2, m, far)), dma((2, m, far))]
    scratch += scatter_scratch(part) + scatter_scratch(part) + scatter_scratch(outs_[0])
    scratch += [
        pltpu.VMEM((tokens, heads_w), BF16),
        pltpu.VMEM(part.shape, BF16),
        pltpu.VMEM((tq, width), F32),
        pltpu.VMEM((2, tq, width // 2), F32),
        pltpu.VMEM((tq, width // 2), F32),
        dma((6,)),
        dma((2,)),
    ]
    return call(body, outs, scratch, args, cid)


def swap_halves(weights):
    w = weights.reshape(weights.shape[0], -1, 2, HEAD_SIZE // 2)
    return jnp.concatenate([-w[:, :, 1:], w[:, :, :1]], axis=2).reshape(weights.shape)


def ordered(r, mine, theirs, axis):
    return jnp.where(
        r == 0,
        jnp.concatenate([mine, theirs], axis=axis),
        jnp.concatenate([theirs, mine], axis=axis),
    )


PAIR = [(0, 1), (1, 0)]


def on_device(
    hidden_in,
    segment_ids,
    position_ids,
    attn_gain,
    query_weight,
    key_weight,
    value_matrix,
    output_weight,
    ffn_gain,
    gate_weight,
    up_weight,
    down_weight,
    out_grad,
):
    r, c = lax.axis_index("row"), lax.axis_index("col")
    t = segment_ids.shape[0]
    width = 2 * hidden_in.shape[1]
    qc, kc = query_weight.shape[1], key_weight.shape[1]
    half = qc % HEAD_SIZE
    fw = gate_weight.shape[1] // 2
    slots_q = (qc + half) // 2
    slots_k = 2 * HEAD_SIZE

    def edge_of(w):
        n = w.shape[1]
        return jnp.where(c == 0, w[:, n - half :], w[:, :half])

    own = jnp.concatenate([query_weight, key_weight, value_matrix], axis=1)
    edge = jnp.concatenate(
        [edge_of(query_weight), edge_of(key_weight), edge_of(value_matrix)], axis=1
    )
    gains = jnp.stack([attn_gain, ffn_gain])
    hid, edge_s, gains, own_s, gate_s, up_s, down_w = exchange(
        ("all", "all", "row", "row", "cols", "cols", "lead"),
        [
            hidden_in,
            edge,
            gains,
            own,
            gate_weight,
            up_weight,
            down_weight.reshape(2, fw, down_weight.shape[1]),
        ],
        1,
        ("square", "", "wide", "", "", "", "wide"),
    )
    output_weight, out_grad, hid = lax.optimization_barrier((output_weight, out_grad, hid))
    wo_x = lax.ppermute(output_weight, "col", PAIR)
    og_x = lax.ppermute(out_grad, "col", PAIR)
    g_one, g_two = gains[0:1], gains[1:2]
    resid = hid.astype(F32)

    frequency = rope_base ** (
        -(jnp.arange(HEAD_SIZE // 2, dtype=F32) * 2.0) / HEAD_SIZE
    )
    angles = position_ids.astype(F32)[:, None] * frequency[None, :]
    cos, sin = jnp.cos(angles), jnp.sin(angles)
    cos = jnp.concatenate([cos, cos], axis=1)
    sin = jnp.concatenate([sin, sin], axis=1)

    own = own_s.reshape(width, qc + 2 * kc)
    edge_x = lax.dynamic_index_in_dim(edge_s, 1 - c, 0, keepdims=False).reshape(width, 3 * half)

    def local(lo, n, e, size):
        ext = ordered(c, own[:, lo : lo + n], edge_x[:, e * half : (e + 1) * half], 1)
        step = (ext.shape[1] - size)
        return lax.dynamic_slice_in_dim(ext, r * step, size, 1)

    wq = local(0, qc, 0, slots_q)
    wk = local(qc, kc, 1, slots_k)
    wv = local(qc + kc, kc, 2, slots_k)
    w_three = jnp.concatenate([wq, wk, wv], axis=1)
    w_all = jnp.concatenate([w_three, swap_halves(wq), swap_halves(wk)], axis=1)
    inv_one = lax.rsqrt(jnp.mean(resid * resid, axis=1, keepdims=True) + epsilon)
    normed_one = (resid * inv_one * g_one).astype(BF16)
    proj = matmul(normed_one, w_all).astype(BF16)
    e1, e2, e3, e4 = slots_q, slots_q + slots_k, slots_q + 2 * slots_k, 2 * slots_q + 2 * slots_k
    q, k, v, qp, kp = proj[:, :e1], proj[:, e1:e2], proj[:, e2:e3], proj[:, e3:e4], proj[:, e4:]
    heads = slots_q // HEAD_SIZE
    group = QUERY_HEADS // KEY_VALUE_HEADS
    first = c * (QUERY_HEADS - 2 * heads) + r * heads
    sel = (first + jnp.arange(heads, dtype=jnp.int32)) // group - first // group
    seg_col, seg_row = segment_ids[:, None], segment_ids[None, :]
    att, lt, qr, qrp, kr, krp = attn_forward(q, k, v, qp, kp, cos, sin, seg_col, seg_row, sel)

    att_all, wo, og = exchange(
        ("all", "row", "row", "row", "row"),
        [att, output_weight, wo_x, out_grad, og_x],
        2,
        ("line", "pair", "-", "pair", "-"),
    )
    wo_pad = jnp.concatenate(
        [wo[: 2 * slots_q], jnp.zeros((HEAD_SIZE, width), BF16), wo[2 * slots_q :]], axis=0
    )
    mid = resid + matmul(att_all, wo_pad)
    inv_two = lax.rsqrt(jnp.mean(mid * mid, axis=1, keepdims=True) + epsilon)
    normed_two = (mid * inv_two * g_two).astype(BF16)
    gate_w = gate_s.reshape(width, fw)
    up_w = up_s.reshape(width, fw)
    gate = matmul(normed_two, gate_w)
    up = matmul(normed_two, up_w)
    sig = jax.nn.sigmoid(gate)
    silu = gate * sig
    inner = (silu * up).astype(BF16)
    inner_grad = contract_cols(og, down_w)
    gate_grad = (inner_grad * up * sig * (1.0 + gate * (1.0 - sig))).astype(BF16)
    up_grad = (inner_grad * silu).astype(BF16)
    both = jnp.concatenate([gate_grad, up_grad], axis=1)
    both_w = jnp.concatenate([gate_w, up_w], axis=1)
    part_two = contract_cols(both, both_w).astype(BF16).reshape(2, 2, t // 4, width)

    slot = 2 * c + r
    def quarter(x):
        return lax.dynamic_slice_in_dim(x, slot * (t // 4), t // 4, 0)

    def row_half(x):
        return lax.dynamic_slice_in_dim(x, r * (width // 2), width // 2, 1)

    hand = jnp.concatenate([both, inner], axis=1)
    hand_x = lax.ppermute(hand, "row", PAIR)
    gate_full = ordered(r, hand[:, :fw], hand_x[:, :fw], 1)
    up_full = ordered(r, hand[:, fw : 2 * fw], hand_x[:, fw : 2 * fw], 1)
    inner_full = ordered(r, hand[:, 2 * fw :], hand_x[:, 2 * fw :], 1)
    n2 = row_half(normed_two)
    n_dp = lax.axis_size("dp")
    gate_wg = contract_rows(gate_full, n2).astype(BF16)
    up_wg = contract_rows(up_full, n2).astype(BF16)
    down_wg = contract_rows(inner_full, row_half(og)).astype(BF16)

    def blocks(x):
        return x.reshape(n_dp, x.shape[0] // n_dp, x.shape[1])

    part_out = jnp.stack(
        [matmul(inner, down_w[:, : width // 2]).astype(BF16), matmul(inner, down_w[:, width // 2 :]).astype(BF16)]
    ).reshape(2, 2, t // 2, width // 2)
    part_out = jnp.transpose(part_out, (1, 0, 2, 3))
    my_mid = lax.dynamic_slice(mid, (c * (t // 2), r * (width // 2)), (t // 2, width // 2))
    wo_mine = lax.dynamic_slice_in_dim(wo_pad, slot * slots_q, slots_q, 0)
    mg_s, gg_two, pg, in_grad, gg_one, hidden_out, down_t, gate_t, up_t = tail(
        [blocks(down_wg), blocks(gate_wg), blocks(up_wg)],
        [part_two, quarter(mid), quarter(og), g_two, wo_mine],
        [qr, qrp, kr, krp, v, lt, att, cos, sin, seg_col, seg_row],
        [w_three, quarter(hid), g_one],
        [part_out, my_mid],
        3,
    )
    mg_all = mg_s.reshape(t, width)
    hidden_in_grad = in_grad.reshape(t // 2, width // 2)

    att15 = jnp.concatenate(
        [att_all[:, : 2 * slots_q], att_all[:, 2 * slots_q + HEAD_SIZE :]], axis=1
    )
    att_c = lax.dynamic_slice_in_dim(att15, c * qc, qc, 1)
    out_wg = contract_rows(att_c, row_half(mg_all))
    pg_x = lax.ppermute(pg, "row", PAIR)
    pg0 = jnp.where(r == 0, pg, pg_x).astype(F32)
    pg1 = jnp.where(r == 0, pg_x, pg).astype(F32)
    ext_q = jnp.concatenate([pg0[:, :e1], pg1[:, :e1]], axis=1)

    def ext_of(lo):
        z = jnp.zeros((t, HEAD_SIZE), F32)
        a, b = pg0[:, lo : lo + slots_k], pg1[:, lo : lo + slots_k]
        return jnp.concatenate([a, z], axis=1) + jnp.concatenate([z, b], axis=1)

    exts = [ext_q, ext_of(e1), ext_of(e2)]
    sends = [jnp.where(c == 0, x[:, -half:], x[:, :half]) for x in exts]
    got = lax.ppermute(jnp.concatenate(sends, axis=1).astype(BF16), "col", PAIR).astype(F32)
    finals = []
    for i, x in enumerate(exts):
        n = x.shape[1]
        g = got[:, i * half : (i + 1) * half]
        low = jnp.concatenate([x[:, : n - 2 * half], x[:, n - 2 * half : n - half] + g], axis=1)
        high = jnp.concatenate([x[:, half : 2 * half] + g, x[:, 2 * half :]], axis=1)
        finals.append(jnp.where(c == 0, low, high).astype(BF16))
    proj_wg = contract_rows(jnp.concatenate(finals, axis=1), row_half(normed_one))
    attn_wg = jnp.concatenate([proj_wg.astype(BF16), out_wg.astype(BF16)], axis=0)
    gain_part = jnp.concatenate([gg_one, gg_two], axis=0)
    attn_t, gain_t = dp_reduce([blocks(attn_wg)], gain_part, 6)
    gain_t = row_half(gain_t)
    attn_t = attn_t.reshape(attn_wg.shape)
    n_proj = qc + 2 * kc
    proj_t = attn_t[:n_proj].T.astype(F32)
    out_t = attn_t[n_proj:]
    gate_t, up_t, down_t = gate_t.T[None], up_t.T[None], down_t[None]
    return (
        hidden_out,
        hidden_in_grad,
        gain_t[0],
        proj_t[:, :qc],
        proj_t[:, qc : qc + kc],
        proj_t[:, qc + kc :],
        out_t.astype(F32),
        gain_t[1],
        gate_t,
        up_t,
        down_t,
    )


def solution(mesh):
    return jax.shard_map(
        on_device,
        mesh=mesh,
        in_specs=(
            P(("dp", "col"), "row"),
            P("dp"),
            P("dp"),
            P("row"),
            P("row", "col"),
            P("row", "col"),
            P("row", "col"),
            P("col", "row"),
            P("row"),
            P("row", "col"),
            P("row", "col"),
            P("col", "row"),
            P(("dp", "col"), "row"),
        ),
        out_specs=(
            P(("dp", "col"), "row"),
            P(("dp", "col"), "row"),
            P("row"),
            P("row", "col"),
            P("row", "col"),
            P("row", "col"),
            P("col", "row"),
            P("row"),
            P("col", "row", "dp"),
            P("col", "row", "dp"),
            P("col", "dp", "row"),
        ),
        check_vma=False,
    )
```
